32 devices in a mesh: wide: 16 (over z, x, core), grp: 2 (over y).
Axes of the slice: x: 2, y: 2, z: 4, core: 2. Of those that a mesh axis runs over, the one named last changes fastest.
Arguments:
- fields: float32 [256, 8, 4096], P('wide', None, 'grp'), may hold values from -6 to 6
- slot_mask: int32 [256, 8], P('wide'), may hold values 0 or 1
- noise_step: int32 [256], P('wide'), may hold values from 0 to 999
- cotangent: bfloat16 [256, 128, 4096], P('wide', 'grp'), may hold values from -6 to 6
- in_weight: float32 [72, 128], replicated, may hold values from -0.75 to 0.75
- in_moment: float32 [72, 128], replicated, may hold values from -6144 to 6144
- in_square: float32 [72, 128], replicated, may hold values from 524288 to 8388608
- mid_weight: float32 [2304, 128], P(('wide', 'grp')), may hold values from -0.1875 to 0.1875
- mid_moment: float32 [2304, 128], P(('wide', 'grp')), may hold values from -2560 to 2560
- mid_square: float32 [2304, 128], P(('wide', 'grp')), may hold values from 83886.08 to 1342177.2
- time_weight: float32 [128, 256], replicated, may hold values from -0.5 to 0.5
- time_moment: float32 [128, 256], replicated, may hold values from -2560 to 2560
- time_square: float32 [128, 256], replicated, may hold values from 83886.08 to 1342177.2
- vec_params: float32 [9, 128], replicated, may hold values from 0.5 to 1.5
- vec_moment: float32 [9, 128], replicated, may hold values from -4096 to 4096
- vec_square: float32 [9, 128], replicated, may hold values from 256901.12 to 4110418
Outputs:
- block_out: float32 [256, 128, 4096], P('wide', 'grp')
- field_grad: float32 [256, 8, 4096], P('wide', None, 'grp')
- in_new: float32 [72, 128], replicated
- in_first: float32 [72, 128], replicated
- in_second: float32 [72, 128], replicated
- in_low: bfloat16 [72, 128], replicated
- mid_new: float32 [2304, 128], P(('wide', 'grp'))
- mid_first: float32 [2304, 128], P(('wide', 'grp'))
- mid_second: float32 [2304, 128], P(('wide', 'grp'))
- mid_low: bfloat16 [2304, 128], P(('wide', 'grp'))
- time_new: float32 [128, 256], replicated
- time_first: float32 [128, 256], replicated
- time_second: float32 [128, 256], replicated
- vec_new: float32 [9, 128], replicated
- vec_first: float32 [9, 128], replicated
- vec_second: float32 [9, 128], replicated
The draws below stay inside these ranges and needn't reach their ends.
All inputs are finite; a program needn't handle non-finite values. No bound on the sum of `slot_mask` on one device may be relied on, other than what follows from the above.
Results may differ from the reference program's by a relative error of at most 0.007.
Values may be sent and summed in bfloat16 or wider, within the bound.
No kernel may reach another device: no remote copies, remote signals or barrier semaphores. Data moves between devices by JAX's collectives and lax.ppermute only.
A program may use at most 512 MiB of HBM per device.

```python
import math
import jax
import jax.numpy as jnp
from jax import lax

C = 128
SLOTS = 8
H = 64
W = 64
TFEAT = 128
TAPS = 9
GROUPS = 8
STEP = 4
IT_DEV = 16
ITEMS = 256
PIX = 4096


def place_ends(entries, own_key, low, largest):
    shape = entries.shape
    place = [jax.random.randint(jax.random.fold_in(own_key, axis), (), 0, shape[axis]) for axis in range(len(shape))]
    entries = entries.at[tuple(place)].set(low)
    longest = shape.index(max(shape))
    place[longest] = (place[longest] + 1) % shape[longest]
    return entries.at[tuple(place)].set(largest)


def block_levels(stream_key, dims, shards, least, high):
    def one(dim, shards_of):
        heights = jax.random.uniform(jax.random.fold_in(jax.random.fold_in(stream_key, 6), dim), (shards_of,), jnp.float32, least / len(shards), high / len(shards))
        return jnp.repeat(jnp.exp(heights), dims[dim] // shards_of).reshape((-1,) + (1,) * (len(dims) - dim - 1))

    gain = one(*shards[0])
    for cut in shards[1:]:
        gain = gain * one(*cut)
    return gain


def centred(own_key, dims, width, bound, shards=(), kind=jnp.bfloat16):
    array = width * jax.random.normal(own_key, dims, jnp.float32)
    if shards:
        array = array * block_levels(own_key, dims, shards, -0.22, 0.18)
    return jnp.clip(array, -bound, bound).astype(kind)


def setup_inputs(seed: int = 0) -> dict:
    splits = jax.random.split(jax.random.key(seed), 17)
    fields = centred(splits[0], (ITEMS, SLOTS, PIX), 1.0, 6.0, ((0, 16), (2, 2)), jnp.float32)
    slot_mask = place_ends((jax.random.randint(splits[1], (ITEMS, SLOTS), 0, 4) < 3).astype(jnp.int32), jax.random.fold_in(splits[1], 1), 0, 1)
    noise_step = place_ends(jax.random.randint(splits[2], (ITEMS,), 0, 1000), jax.random.fold_in(splits[2], 1), 0, 999).astype(jnp.int32)
    cotangent = centred(splits[3], (ITEMS, C, PIX), 1.0, 6.0, ((0, 16), (1, 2)))
    in_weight = centred(splits[4], (TAPS * SLOTS, C), (TAPS * SLOTS) ** -0.5, 0.75, (), jnp.float32)
    in_moment = centred(splits[5], (TAPS * SLOTS, C), ((ITEMS * PIX) ** 0.5), 6144.0, (), jnp.float32)
    in_square = jnp.clip(jnp.exp(jax.random.uniform(splits[6], (TAPS * SLOTS, C), jnp.float32, math.log(524288.0), math.log(8388608))), 524288.0, 8388608)
    mid_weight = centred(splits[7], (2 * TAPS * C, C), (TAPS * C) ** -0.5, 0.1875, ((0, 32),), jnp.float32)
    mid_moment = centred(splits[8], (2 * TAPS * C, C), (0.4 * (ITEMS * PIX) ** 0.5), 2560.0, ((0, 32),), jnp.float32)
    mid_square = jnp.clip(jnp.exp(math.log(1342177.2) - 2.7725887 * jax.random.uniform(splits[9], (2 * TAPS * C, C), jnp.float32) ** block_levels(splits[9], (2 * TAPS * C, C), ((0, 32),), -0.2, 0.2)), 83886.08, 1342177.2)
    time_weight = centred(splits[10], (TFEAT, 2 * C), TFEAT ** -0.5, 0.5, (), jnp.float32)
    time_moment = centred(splits[11], (TFEAT, 2 * C), (0.4 * (ITEMS * PIX) ** 0.5), 2560.0, (), jnp.float32)
    time_square = jnp.clip(jnp.exp(jax.random.uniform(splits[12], (TFEAT, 2 * C), jnp.float32, math.log(83886.08), math.log(1342177.2))), 83886.08, 1342177.2)
    vec_params = jnp.clip(jax.random.uniform(splits[13], (9, C), jnp.float32, 0.5, 1.5), 0.5, 1.5)
    vec_moment = centred(splits[14], (9, C), (0.7 * (ITEMS * PIX) ** 0.5), 4096.0, (), jnp.float32)
    vec_square = jnp.clip(jnp.exp(jax.random.uniform(splits[15], (9, C), jnp.float32, math.log(256901.12), math.log(4110418))), 256901.12, 4110418)
    return {"fields": fields, "slot_mask": slot_mask, "noise_step": noise_step, "cotangent": cotangent, "in_weight": in_weight, "in_moment": in_moment, "in_square": in_square, "mid_weight": mid_weight, "mid_moment": mid_moment, "mid_square": mid_square, "time_weight": time_weight, "time_moment": time_moment, "time_square": time_square, "vec_params": vec_params, "vec_moment": vec_moment, "vec_square": vec_square}


@jax.custom_vjp
def low(v):
    return lax.optimization_barrier(v.astype(jnp.bfloat16)).astype(jnp.float32)

@jax.custom_vjp
def low_back(v):
    return v

def low_keep(v):
    return (low(v), None)

def low_pass(kept, grad):
    return (grad,)

def back_keep(v):
    return (v, None)

def back_low(kept, grad):
    return (low(grad),)
low.defvjp(low_keep, low_pass)
low_back.defvjp(back_keep, back_low)
highest = lax.Precision.HIGHEST
beta_one = 0.5
beta_two = 0.5
epsilon = 1e-08
weight_decay = 0.01
rate_in = 0.1
rate_mid = 0.03
rate_time = 0.1
rate_vecs = 0.3
norm_epsilon = 1e-05

def fourier(noise_step, feature_count):
    half_count = feature_count // 2
    frequency = jnp.exp(-math.log(10000.0) * jnp.arange(half_count, dtype=jnp.float32) / half_count)
    angles = noise_step.astype(jnp.float32)[:, None] * frequency[None, :]
    return jnp.concatenate([jnp.sin(angles), jnp.cos(angles)], axis=1)

def conv_full(values, taps):
    running = 0.0
    for row_shift in range(3):
        for col_shift in range(3):
            shifted = jnp.roll(values, (1 - row_shift, 1 - col_shift), axis=(2, 3))
            running = running + jnp.einsum('nchw,cd->ndhw', shifted, taps[row_shift * 3 + col_shift], precision=highest)
    return running

def group_norm(values, gain_vec, beta_vec, group_width):
    item_count, chans, cells = values.shape
    grouped = values.reshape(item_count, chans // group_width, group_width * cells)
    group_mean = lax.optimization_barrier(jnp.mean(grouped, axis=2, keepdims=True))
    centered = grouped - group_mean
    group_var = lax.optimization_barrier(jnp.mean(centered * centered, axis=2, keepdims=True))
    normed = (centered * lax.rsqrt(group_var + norm_epsilon)).reshape(item_count, chans, cells)
    return normed * gain_vec[None, :, None] + beta_vec[None, :, None]

def adam_update(weight, grad, moment, square, rate, step_float):
    moment_new = beta_one * moment + (1.0 - beta_one) * grad
    square_new = beta_two * square + (1.0 - beta_two) * grad * grad
    moment_hat = moment_new / (1.0 - jnp.power(beta_one, step_float))
    square_hat = square_new / (1.0 - jnp.power(beta_two, step_float))
    weight_new = weight - rate * (moment_hat / (jnp.sqrt(square_hat) + epsilon) + weight_decay * weight)
    return (weight_new, moment_new, square_new)

def forward(field_block, mask_block, features, in_weight, mid_weight, time_weight, vec_params):
    group_width = C // GROUPS
    masked_low = low(field_block * mask_block[:, :, None]).reshape(-1, SLOTS, H, W)
    input_taps = low(in_weight).reshape(TAPS, SLOTS, C)
    inner_taps = low(mid_weight).reshape(2, TAPS, C, C)
    lifted = low_back(low(conv_full(masked_low, input_taps))).reshape(-1, C, PIX)
    hidden = lifted + vec_params[0][None, :, None]
    first_act = low_back(low(jax.nn.gelu(group_norm(hidden, vec_params[1], vec_params[2], group_width))))
    first_conv = low_back(low(conv_full(first_act.reshape(-1, C, H, W), inner_taps[0]))).reshape(-1, C, PIX)
    scaling = jnp.dot(features, time_weight[:, :C], precision=highest) + vec_params[4][None, :]
    offset = jnp.dot(features, time_weight[:, C:], precision=highest) + vec_params[5][None, :]
    modulated = (first_conv + vec_params[3][None, :, None]) * (1.0 + scaling[:, :, None]) + offset[:, :, None]
    second_act = low_back(low(jax.nn.gelu(group_norm(modulated, vec_params[6], vec_params[7], group_width))))
    second_conv = low_back(low(conv_full(second_act.reshape(-1, C, H, W), inner_taps[1]))).reshape(-1, C, PIX)
    return hidden + second_conv + vec_params[8][None, :, None]

def reference(fields, slot_mask, noise_step, cotangent, in_weight, in_moment, in_square, mid_weight, mid_moment, mid_square, time_weight, time_moment, time_square, vec_params, vec_moment, vec_square):
    block_items = min(IT_DEV, 8)
    block_total = ITEMS // block_items
    features_all = fourier(noise_step, TFEAT)
    mask_all = slot_mask.astype(jnp.float32)
    cot_all = cotangent.astype(jnp.float32)

    def run_block(totals, block_index):
        first_item = (block_index * block_items).astype(jnp.int32)
        field_block = lax.dynamic_slice_in_dim(fields, first_item, block_items, 0)
        mask_block = lax.dynamic_slice_in_dim(mask_all, first_item, block_items, 0)
        feature_block = lax.dynamic_slice_in_dim(features_all, first_item, block_items, 0)
        cot_block = lax.dynamic_slice_in_dim(cot_all, first_item, block_items, 0)

        def local_forward(field_part, weight_in, weight_mid, weight_time, weight_vecs):
            return forward(field_part, mask_block, feature_block, weight_in, weight_mid, weight_time, weight_vecs)
        out_block, pullback = jax.vjp(local_forward, field_block, in_weight, mid_weight, time_weight, vec_params)
        gradients = pullback(cot_block)
        totals = tuple((held + fresh for held, fresh in zip(totals, gradients[1:])))
        return (totals, (out_block, gradients[0]))
    start_totals = (jnp.zeros_like(in_weight), jnp.zeros_like(mid_weight), jnp.zeros_like(time_weight), jnp.zeros_like(vec_params))
    totals, stacked = lax.scan(run_block, start_totals, jnp.arange(block_total, dtype=jnp.int32))
    block_out = stacked[0].reshape(ITEMS, C, PIX)
    field_grad = stacked[1].reshape(ITEMS, SLOTS, PIX)
    step_float = jnp.float32(STEP)
    in_new, in_first, in_second = adam_update(in_weight, totals[0], in_moment, in_square, rate_in, step_float)
    mid_new, mid_first, mid_second = adam_update(mid_weight, totals[1], mid_moment, mid_square, rate_mid, step_float)
    time_new, time_first, time_second = adam_update(time_weight, totals[2], time_moment, time_square, rate_time, step_float)
    vec_new, vec_first, vec_second = adam_update(vec_params, totals[3], vec_moment, vec_square, rate_vecs, step_float)
    return (block_out, field_grad, in_new, in_first, in_second, in_new.astype(jnp.bfloat16), mid_new, mid_first, mid_second, mid_new.astype(jnp.bfloat16), time_new, time_first, time_second, vec_new, vec_first, vec_second)
```

```python
import functools
import math

import jax
import jax.numpy as jnp
from jax import lax
from jax.experimental import pallas as pl
from jax.experimental.pallas import tpu as pltpu
from jax.sharding import PartitionSpec as P

C = 128
W = 64
H = 64
PIX = H * W
TAPS = 9
GROUPS = 8
STEP = 4
NJ = 4
NS = W // NJ
ROWS = H * NS

highest = lax.Precision.HIGHEST
beta_one = 0.5
beta_two = 0.5
epsilon = 1e-08
weight_decay = 0.01
rate_in = 0.1
rate_mid = 0.03
rate_time = 0.1
rate_vecs = 0.3
norm_epsilon = 1e-05
bf = jnp.bfloat16
f32 = jnp.float32
GELU_C = math.sqrt(2.0 / math.pi)
GELU_K = 0.044715
VMEM_LIMIT = 58 << 20


def fourier(noise_step, feature_count):
    half_count = feature_count // 2
    frequency = jnp.exp(-math.log(10000.0) * jnp.arange(half_count, dtype=jnp.float32) / half_count)
    angles = noise_step.astype(jnp.float32)[:, None] * frequency[None, :]
    return jnp.concatenate([jnp.sin(angles), jnp.cos(angles)], axis=1)


def adam_update(weight, grad, moment, square, rate, step_float):
    moment_new = beta_one * moment + (1.0 - beta_one) * grad
    square_new = beta_two * square + (1.0 - beta_two) * grad * grad
    moment_hat = moment_new / (1.0 - jnp.power(beta_one, step_float))
    square_hat = square_new / (1.0 - jnp.power(beta_two, step_float))
    weight_new = weight - rate * (
        moment_hat / (jnp.sqrt(square_hat) + epsilon) + weight_decay * weight
    )
    return (weight_new, moment_new, square_new)


def group_sum(v):
    lane = lax.broadcasted_iota(jnp.int32, v.shape, 1)
    for k in (1, 2, 4, 8):
        v = v + jnp.where((lane & k) == 0, pltpu.roll(v, C - k, 1), pltpu.roll(v, k, 1))
    return v


def rows8(v):
    return jnp.sum(v.reshape(v.shape[0] // 8, 8, v.shape[1]), axis=0)


def gelu(x):
    x2 = x * x
    t = jnp.tanh(x * (GELU_C + (GELU_C * GELU_K) * x2))
    h = 0.5 * x
    return h + h * t


def gelu_slope(x):
    x2 = x * x
    t = jnp.tanh(x * (GELU_C + (GELU_C * GELU_K) * x2))
    q = (0.5 * GELU_C) + (1.5 * GELU_C * GELU_K) * x2
    return (0.5 + 0.5 * t) + (x * q) * (1.0 - t * t)


def band_weights(k_ref, t_ref, adjoint):
    zero = jnp.zeros((C, C), bf)
    for a in range(3):
        for m in range(4):
            row = (a * 4 + m) * C
            for par in range(2):
                b = m - par
                if 0 <= b <= 2:
                    if adjoint:
                        block = k_ref[(2 - a) * 3 + (2 - b)].T
                    else:
                        block = k_ref[a * 3 + b]
                else:
                    block = zero
                t_ref[row : row + C, par * C : (par + 1) * C] = block


def put_padded(p_ref, j, v, y0, count):
    vb = v.astype(bf).reshape(count, NS, C)
    spots = [(j + 1, vb)]
    if j == NJ - 1:
        spots.append((0, pltpu.roll(v.reshape(count, NS, C), 1, 1).astype(bf)))
    if j == 0:
        spots.append((NJ + 1, pltpu.roll(v.reshape(count, NS, C), NS - 1, 1).astype(bf)))
    for slot, value in spots:
        p_ref[slot, pl.ds(y0 + 1, count)] = value
    return vb


def wrap_rows(p_ref):
    for slot in range(NJ + 2):
        p_ref[slot, 0] = p_ref[slot, H]
        p_ref[slot, H + 1] = p_ref[slot, 1]


def piece(p_ref, slot, a, y0, count):
    return p_ref[slot, pl.ds(a + y0, count)].reshape(count * NS, C)


def conv_rows(p_ref, t_ref, q, y0, count):
    left = jnp.concatenate(
        [piece(p_ref, 2 * q + m, a, y0, count) for a in range(3) for m in range(4)], axis=1
    )
    return jnp.dot(left, t_ref[...], preferred_element_type=f32)


def run(main, *others):
    main = list(main)
    rest = [step for other in others for step in other]
    done = 0
    for i, step in enumerate(main):
        step()
        upto = (i + 1) * len(rest) // len(main)
        for other in rest[done:upto]:
            other()
        done = upto


def weight_grad(xt_ref, at, p_ref, acc_ref, which):
    def step(a, n):
        total = None
        for q in range(2):
            right = jnp.concatenate(
                [piece(p_ref, 2 * q + 2 * n + m, a, 0, H) for m in range(2)], axis=1
            )
            part = jnp.dot(xt_ref[at, q], right, preferred_element_type=f32)
            total = part if total is None else total + part
        acc_ref[which, a, :, n * 2 * C : (n + 1) * 2 * C] += total

    return [functools.partial(step, a, n) for a in range(3) for n in range(2)]


def emit_weight_grad(acc_ref, which, out_ref):
    for a in range(3):
        for b in range(3):
            total = None
            for par in range(2):
                m = par + 2 - b
                block = acc_ref[which, 2 - a, par * C : (par + 1) * C, m * C : (m + 1) * C]
                total = block if total is None else total + block
            out_ref[which, (a * 3 + b) * C : (a * 3 + b + 1) * C, :] = total


def finish_stats(s1, s2, shift, alpha, bias, extra):
    inv = 1.0 / PIX
    s1 = jnp.sum(s1, axis=0, keepdims=True) * inv
    s2 = jnp.sum(s2, axis=0, keepdims=True) * inv
    mean = shift + s1
    var = jnp.maximum(s2 - s1 * s1, 0.0)
    mean_v = alpha * (mean + bias) + extra
    mu = group_sum(mean_v) * (1.0 / 16)
    centred = mean_v - mu
    group_var = group_sum(alpha * alpha * var + centred * centred) * (1.0 / 16)
    rstd = lax.rsqrt(group_var + norm_epsilon)
    return mean, var, mean_v, mu, rstd


def pick(index, options):
    chosen = options[0]
    for k in range(1, len(options)):
        chosen = jnp.where(index == k, options[k], chosen)
    return chosen


def chunks(count):
    return [(j, y0) for j in range(NJ) for y0 in range(0, H, count)]


def forward_kernel(
    groups,
    me_ref,
    *refs,
):
    f_refs, refs = refs[:groups], refs[groups:]
    forward_items(groups, me_ref[0], f_refs, *refs)


def forward_items(
    groups,
    me,
    f_refs,
    perm_ref,
    tin_ref,
    k_ref,
    vec_ref,
    item_ref,
    lifted_ref,
    conv_ref,
    x1t_ref,
    x2t_ref,
    im_ref,
    stat_ref,
    *rest,
):
    out_refs, scratch = rest[:groups], rest[groups:]
    t1_ref, t2_ref = scratch[:2]
    pads = (scratch[2:4], scratch[4:6])
    z_refs = scratch[6:8]
    own = C // groups

    @pl.when(pl.program_id(0) == 0)
    def _():
        band_weights(k_ref.at[0], t1_ref, False)
        band_weights(k_ref.at[1], t2_ref, False)

    def vec(i):
        return vec_ref[i : i + 1, :]

    def item(n):
        state = {}
        p1_ref, p2_ref = pads[n]
        z_ref = z_refs[n]

        def lift():
            parts = [ref[n].astype(f32) for ref in f_refs]
            raw = jnp.concatenate(
                [
                    pick(me, [parts[(g - k) % groups] for g in range(groups)])
                    for k in range(groups)
                ],
                axis=1,
            )
            rows = jnp.concatenate([raw[:, i * 512 : (i + 1) * 512] for i in range(8)], axis=0)
            spread = jnp.dot(rows.astype(bf), perm_ref[...], preferred_element_type=f32)
            lane = lax.broadcasted_iota(jnp.int32, (64, 128), 1) % NS
            cols = [spread[:, j * 128 : (j + 1) * 128] for j in range(NJ)]
            before = jnp.where(
                lane == 0, pltpu.roll(cols[3], 128 - 15, 1), pltpu.roll(cols[3], 1, 1)
            )
            after = jnp.where(
                lane == NS - 1, pltpu.roll(cols[0], 15, 1), pltpu.roll(cols[0], 127, 1)
            )
            taps = []
            for v in [before] + cols + [after]:
                taps.append(jnp.concatenate([v[i * 8 : (i + 1) * 8, :] for i in range(8)], axis=1))
            stack = jnp.concatenate(taps, axis=0)
            up = pltpu.roll(stack, NS, 1)
            down = pltpu.roll(stack, ROWS - NS, 1)
            im_ref[n] = jnp.concatenate([up, stack, down], axis=0).astype(bf)

        def clear():
            state["s1"] = jnp.zeros((8, C), f32)
            state["s2"] = jnp.zeros((8, C), f32)
            state["shift"] = None

        def gather_stats(x):
            if state["shift"] is None:
                state["shift"] = x[0:1, :]
            x = x - state["shift"]
            state["s1"] = state["s1"] + rows8(x)
            state["s2"] = state["s2"] + rows8(x * x)

        def conv_in(part):
            if part == 0:
                clear()
            left = im_ref[n, :, part * 256 : (part + 1) * 256]
            r = lax.dot_general(
                left, tin_ref[...], (((0,), (0,)), ((), ())), preferred_element_type=f32
            )
            for j in range(NJ):
                x = r[:, j * C : (j + 1) * C]
                lifted_ref[n, j, part * 256 : (part + 1) * 256, :] = x.astype(bf)
                gather_stats(x)

        def first_stats():
            one = jnp.ones((1, C), f32)
            zero = jnp.zeros((1, C), f32)
            mean, var, mean_v, mu, rstd = finish_stats(
                state["s1"], state["s2"], state["shift"], one, vec(0), zero
            )
            state["scale"] = rstd * vec(1)
            state["base"] = (mean_v - mu - mean) * state["scale"] + vec(2)
            state["one"] = [mean, var, mu, rstd]

        def normal(src_ref, p_ref, xt_ref, count, j, y0):
            at = slice(y0 * NS, (y0 + count) * NS)
            x = src_ref[n, j, at, :].astype(f32)
            v = gelu(x * state["scale"] + state["base"])
            vb = put_padded(p_ref, j, v, y0, count)
            xt_ref[n, j // 2, (j % 2) * C : (j % 2 + 1) * C, at] = vb.reshape(count * NS, C).T

        def conv_one(q, y0, count):
            if q == 0 and y0 == 0:
                clear()
            r = conv_rows(p1_ref, t1_ref, q, y0, count)
            for par in range(2):
                x = r[:, par * C : (par + 1) * C]
                conv_ref[n, 2 * q + par, y0 * NS : (y0 + count) * NS, :] = x.astype(bf)
                gather_stats(x)

        def second_stats():
            alpha = item_ref[n, 0:1, :]
            extra = item_ref[n, 1:2, :]
            mean, var, mean_v, mu, rstd = finish_stats(
                state["s1"], state["s2"], state["shift"], alpha, vec(3), extra
            )
            state["scale"] = rstd * alpha * vec(6)
            state["base"] = (mean_v - mu) * rstd * vec(6) - mean * state["scale"] + vec(7)
            stat_ref[n] = jnp.concatenate(state["one"] + [mean, var, mu, rstd], axis=0)

        def conv_two(q, y0, count):
            r = conv_rows(p2_ref, t2_ref, q, y0, count)
            add = vec(0) + vec(8)
            for par in range(2):
                j = 2 * q + par
                at = slice(y0 * NS, (y0 + count) * NS)
                x = r[:, par * C : (par + 1) * C] + lifted_ref[n, j, at, :].astype(f32) + add
                z_ref[pl.ds(y0 * W + j, count * NS, stride=NJ), :] = x

        def flip(i):
            at = slice(i * 128, (i + 1) * 128)
            t = z_ref[at, :].T
            for s in range(groups):
                chans = [(g + s) % groups * own for g in range(groups)]
                piece = pick(me, [t[c : c + own, :] for c in chans])
                out_refs[s][n, :, at] = piece.astype(out_refs[s].dtype)

        part = functools.partial
        small, big = 8, 16
        bands = [(q, y0) for q in range(2) for y0 in range(0, H, big)]
        return {
            "lift": [lift] + [part(conv_in, k) for k in range(4)] + [first_stats],
            "one": [part(normal, lifted_ref, p1_ref, x1t_ref, small, *c) for c in chunks(small)]
            + [part(wrap_rows, p1_ref)],
            "conv1": [part(conv_one, *b, big) for b in bands] + [second_stats],
            "two": [part(normal, conv_ref, p2_ref, x2t_ref, small, *c) for c in chunks(small)]
            + [part(wrap_rows, p2_ref)],
            "conv2": [part(conv_two, *b, big) for b in bands],
            "flip": [part(flip, i) for i in range(PIX // 128)],
        }

    a, b = item(0), item(1)
    run(a["lift"])
    run(a["one"])
    run(a["conv1"], b["lift"], b["one"])
    run(b["conv1"], a["two"])
    run(a["conv2"], b["two"])
    run(b["conv2"], a["flip"])
    run(b["flip"])


def first_back_kernel(groups, items, chained, me_ref, *refs):
    step = pl.program_id(0)
    me = me_ref[0]
    start_refs, refs = refs[:groups], refs[groups:]
    next_refs, refs = refs[:groups], refs[groups:]
    conv_ref, x1t_ref, x2t_ref, stat_ref, item_ref, vec_ref, k_ref = refs[:7]
    refs = refs[7:]
    if chained:
        before_ref, refs = refs[2], refs[3:]
    pc_ref, pd_ref, dk_ref, dvec_ref, ditem_ref, t2_ref, z_ref, d_ref, acc_ref = refs
    pc_ref, pd_ref = pc_ref.at[0], pd_ref.at[0]
    part = functools.partial
    small, big = 8, 16

    def flip(src_refs, i):
        at = slice(i * 128, (i + 1) * 128)
        parts = [ref[0, :, at] for ref in src_refs]
        t = jnp.concatenate(
            [pick(me, [parts[(g - k) % groups] for g in range(groups)]) for k in range(groups)],
            axis=0,
        )
        z_ref[at, :] = t.astype(f32).T

    @pl.when(step == 0)
    def _():
        band_weights(k_ref.at[1], t2_ref, True)
        acc_ref[...] = jnp.zeros_like(acc_ref)
        dvec_ref[...] = jnp.zeros_like(dvec_ref)
        run([part(flip, start_refs, i) for i in range(PIX // 128)])

    def vec(i):
        return vec_ref[i : i + 1, :]

    def stat(i):
        return stat_ref[0, i : i + 1, :]

    cot_sum = jnp.zeros((8, C), f32)
    for j, y0 in chunks(big):
        v = z_ref[pl.ds(y0 * W + j, big * NS, stride=NJ), :]
        cot_sum = cot_sum + rows8(v)
        put_padded(pc_ref, j, v, y0, big)
    cot_sum = jnp.sum(cot_sum, axis=0, keepdims=True)
    wrap_rows(pc_ref)

    alpha = item_ref[0, 0:1, :]
    extra = item_ref[0, 1:2, :]
    mean, var, mu, rstd = stat(4), stat(5), stat(6), stat(7)
    mean_v = alpha * (mean + vec(3)) + extra
    sb, sx, sg, mean_en, c1, c2, c3, total = norm_back(
        pc_ref, t2_ref, conv_ref, d_ref, mean, mean_v, mu, rstd, alpha, vec(6), vec(7)
    )
    d_scaling = (
        rstd * (vec(6) * sx - mean_en * (rstd * alpha * PIX) * var) + (mean + vec(3)) * total
    )
    ditem_ref[0] = jnp.concatenate([d_scaling, total, jnp.zeros((6, C), f32)], axis=0)
    zero = jnp.zeros((1, C), f32)
    dvec_ref[...] += jnp.concatenate(
        [alpha * total, d_scaling, total, sg, sb, cot_sum, zero, zero], axis=0
    )

    def spread(j, y0):
        at = slice(y0 * NS, (y0 + small) * NS)
        x = conv_ref[0, j, at, :].astype(f32) - mean
        put_padded(pd_ref, j, d_ref[j, at, :] * c1 + (x * c3 + c2), y0, small)

    run(
        weight_grad(x2t_ref, 0, pc_ref, acc_ref, 1),
        [part(spread, *c) for c in chunks(small)],
    )
    wrap_rows(pd_ref)
    run(
        weight_grad(x1t_ref, 0, pd_ref, acc_ref, 0),
        [part(flip, next_refs, i) for i in range(PIX // 128)],
    )

    @pl.when(step == items - 1)
    def _():
        emit_weight_grad(acc_ref, 0, dk_ref)
        emit_weight_grad(acc_ref, 1, dk_ref)
        if chained:
            dk_ref[...] += before_ref[...]


def norm_back(p_ref, t_ref, src_ref, d_ref, mean, mean_v, mu, rstd, alpha, gain, beta):
    big = 16
    slope = rstd * alpha
    centre = (mean_v - mu) * rstd
    scale = slope * gain
    base = centre * gain + beta
    sums = [jnp.zeros((8, C), f32), jnp.zeros((8, C), f32)]

    def conv(q, y0):
        r = conv_rows(p_ref, t_ref, q, y0, big)
        for par in range(2):
            j = 2 * q + par
            at = slice(y0 * NS, (y0 + big) * NS)
            x = src_ref[0, j, at, :].astype(f32) - mean
            d = r[:, par * C : (par + 1) * C] * gelu_slope(x * scale + base)
            d_ref[j, at, :] = d
            sums[0] = sums[0] + rows8(d)
            sums[1] = sums[1] + rows8(d * x)

    run([functools.partial(conv, q, y0) for q in range(2) for y0 in range(0, H, big)])
    sb = jnp.sum(sums[0], axis=0, keepdims=True)
    sx = jnp.sum(sums[1], axis=0, keepdims=True)
    sg = slope * sx + centre * sb
    inv = 1.0 / (16 * PIX)
    mean_e = group_sum(gain * sb) * inv
    mean_en = group_sum(gain * sg) * inv
    c1 = slope * gain
    c3 = -slope * slope * mean_en
    c2 = -slope * (mean_e + mean_en * centre)
    total = rstd * (gain * sb - PIX * mean_e - PIX * mean_en * centre)
    return sb, sx, sg, mean_en, c1, c2, c3, total


def second_back_kernel(
    groups,
    pc_ref,
    pd_ref,
    lifted_ref,
    im_ref,
    stat_ref,
    vec_ref,
    tin_ref,
    perm_ref,
    k_ref,
    field_ref,
    din_ref,
    dvec_ref,
    t1_ref,
    d_ref,
    low_ref,
):
    small = 8
    pc_ref, pd_ref = pc_ref.at[0], pd_ref.at[0]

    @pl.when(pl.program_id(0) == 0)
    def _():
        band_weights(k_ref.at[0], t1_ref, True)
        din_ref[...] = jnp.zeros_like(din_ref)
        dvec_ref[...] = jnp.zeros_like(dvec_ref)

    def vec(i):
        return vec_ref[i : i + 1, :]

    def stat(i):
        return stat_ref[0, i : i + 1, :]

    one = jnp.ones((1, C), f32)
    mean, mu, rstd = stat(0), stat(2), stat(3)
    sb, sx, sg, mean_en, c1, c2, c3, total = norm_back(
        pd_ref, t1_ref, lifted_ref, d_ref, mean, mean + vec(0), mu, rstd, one, vec(1), vec(2)
    )
    for j, y0 in chunks(small):
        at = slice(y0 * NS, (y0 + small) * NS)
        x = lifted_ref[0, j, at, :].astype(f32) - mean
        g = pc_ref[j + 1, y0 + 1 : y0 + 1 + small].reshape(small * NS, C).astype(f32)
        low_ref[at, j * C : (j + 1) * C] = (g + (d_ref[j, at, :] * c1 + (x * c3 + c2))).astype(bf)
    dvec_ref[...] += jnp.concatenate([total, sg, sb, jnp.zeros((5, C), f32)], axis=0)

    din_ref[...] += jnp.dot(im_ref[0], low_ref[...], preferred_element_type=f32)
    back = lax.dot_general(
        tin_ref[...], low_ref[...], (((1,), (1,)), ((), ())), preferred_element_type=f32
    )
    stack = (
        pltpu.roll(back[0:48], ROWS - NS, 1) + back[48:96] + pltpu.roll(back[96:144], NS, 1)
    )
    lane = lax.broadcasted_iota(jnp.int32, (64, 128), 1) % NS

    def tall(jj):
        v = stack[jj * 8 : (jj + 1) * 8, :]
        return jnp.concatenate([v[:, i * 128 : (i + 1) * 128] for i in range(8)], axis=0)

    before, after = tall(0), tall(NJ + 1)
    before = jnp.where(lane == NS - 1, pltpu.roll(before, 15, 1), pltpu.roll(before, 127, 1))
    after = jnp.where(lane == 0, pltpu.roll(after, 128 - 15, 1), pltpu.roll(after, 1, 1))
    cols = [tall(j + 1) for j in range(NJ)]
    cols[3] = cols[3] + before
    cols[0] = cols[0] + after
    rows = jnp.concatenate(cols, axis=1).astype(bf)
    spread = lax.dot_general(
        rows, perm_ref[...], (((1,), (1,)), ((), ())), preferred_element_type=f32
    )
    natural = jnp.concatenate([spread[i * 8 : (i + 1) * 8, :] for i in range(8)], axis=1)
    cells = PIX // groups
    for g in range(groups):
        field_ref[g, 0] = natural[:, g * cells : (g + 1) * cells].astype(bf)


def whole(shape):
    return pl.BlockSpec(shape, lambda i, *_: (0,) * len(shape))


def by_item(shape, count=1, start=0):
    return pl.BlockSpec((count,) + shape, lambda i, *_: (i + start,) + (0,) * len(shape))


def swap(x, axis, hops):
    size = lax.axis_size(axis)
    return lax.ppermute(x, axis, [(i, (i + hops) % size) for i in range(size)])


def all_sum(x, axes):
    for axis in axes:
        size = lax.axis_size(axis)
        bit = 1
        while bit < size:
            x = x + lax.ppermute(x, axis, [(i, i ^ bit) for i in range(size)])
            bit *= 2
    return x


def local(
    fields,
    slot_mask,
    noise_step,
    cotangent,
    in_weight,
    in_moment,
    in_square,
    mid_weight,
    mid_moment,
    mid_square,
    time_weight,
    time_moment,
    time_square,
    vec_params,
    vec_moment,
    vec_square,
):
    both = ("wide", "grp")
    groups = lax.axis_size("grp")
    devices = groups * lax.axis_size("wide")
    held = fields.shape[0]
    items = held // groups
    slots = fields.shape[1]
    own = cotangent.shape[1]
    cells = fields.shape[2]
    me = lax.axis_index("grp")
    first_item = me * items
    pair = 2
    halves = 2
    some = items // halves

    mask_float = slot_mask.astype(f32)[:, :, None]
    masked_low = (fields * mask_float).astype(bf)

    def to_peer(x, hops, start, count):
        at = lax.rem(me + hops, groups) * items + start
        return swap(lax.dynamic_slice_in_dim(x, at, count, 0), "grp", hops)

    field_parts = [masked_low] + [to_peer(masked_low, s, 0, items) for s in range(1, groups)]
    share = mid_weight.shape[0]
    copies = jnp.broadcast_to(mid_weight.astype(bf)[None], (devices, share, C))
    gathered = lax.all_to_all(copies, both, split_axis=0, concat_axis=0, tiled=True)
    inner_taps = gathered.reshape(2, TAPS, C, C)
    cot_parts = [
        [to_peer(cotangent, s, h * some, some) for s in range(1, groups)] for h in range(halves)
    ]

    taps_in = in_weight.astype(bf).reshape(3, 3, slots, C)
    tin = jnp.stack(
        [jnp.pad(taps_in, ((0, 0), (j, NJ - 1 - j), (0, 0), (0, 0))) for j in range(NJ)], axis=3
    ).reshape(3 * (NJ + 2) * slots, NJ * C)
    spot = jnp.arange(8 * W)
    goal = (spot % NJ) * 128 + (spot // W) * NS + (spot % W) // NJ
    perm = (goal[:, None] == spot[None, :]).astype(bf)

    steps = lax.dynamic_slice_in_dim(noise_step, first_item, items, 0)
    features = fourier(steps, time_weight.shape[0])
    scaling = jnp.dot(features, time_weight[:, :C], precision=highest) + vec_params[4][None, :]
    offset = jnp.dot(features, time_weight[:, C:], precision=highest) + vec_params[5][None, :]
    item_vec = jnp.stack([1.0 + scaling, offset] + [jnp.zeros_like(offset)] * 6, axis=1)
    vecs = jnp.pad(vec_params, ((0, 7), (0, 0)))

    act = jax.ShapeDtypeStruct((items, NJ, ROWS, C), bf)
    flat = jax.ShapeDtypeStruct((items, 2, 2 * C, ROWS), bf)
    taps_rows = 3 * (NJ + 2) * slots
    pad_shape = (NJ + 2, H + 2, NS, C)
    pads = jax.ShapeDtypeStruct((items,) + pad_shape, bf)
    row = jax.ShapeDtypeStruct((items, 8, C), f32)
    band = pltpu.VMEM((12 * C, 2 * C), bf)
    tall = pltpu.VMEM((PIX, C), f32)
    params = pltpu.CompilerParams(vmem_limit_bytes=VMEM_LIMIT)
    my_group = me.astype(jnp.int32).reshape(1)

    def work(count, size, moved):
        gain = 2 * TAPS * C * C * PIX
        return pl.CostEstimate(
            flops=int(count * size * gain * 2),
            bytes_accessed=int(count * moved * 2 * C * PIX),
            transcendentals=0,
        )

    def mine(shape, count, index):
        return pl.BlockSpec(
            (count,) + shape, lambda i, g: (g[0] * (items // count) + index(i), 0, 0)
        )

    lifted, first_conv, x1t, x2t, im, stats, block_out, *sends = pl.pallas_call(
        functools.partial(forward_kernel, groups),
        grid_spec=pltpu.PrefetchScalarGridSpec(
            num_scalar_prefetch=1,
            grid=(items // pair,),
            in_specs=[mine((slots, cells), pair, lambda i: i)]
            + [by_item((slots, cells), pair)] * (groups - 1)
            + [
                whole((8 * W, 8 * W)),
                whole((taps_rows, NJ * C)),
                whole((2, TAPS, C, C)),
                whole((16, C)),
                by_item((8, C), pair),
            ],
            out_specs=[
                by_item((NJ, ROWS, C), pair),
                by_item((NJ, ROWS, C), pair),
                by_item((2, 2 * C, ROWS), pair),
                by_item((2, 2 * C, ROWS), pair),
                by_item((taps_rows, ROWS), pair),
                by_item((8, C), pair),
                mine((own, PIX), pair, lambda i: i),
            ]
            + [by_item((own, PIX), pair)] * (groups - 1),
            scratch_shapes=[band] * 2 + [pltpu.VMEM(pad_shape, bf)] * 4 + [tall] * 2,
        ),
        out_shape=[
            act,
            act,
            flat,
            flat,
            jax.ShapeDtypeStruct((items, taps_rows, ROWS), bf),
            row,
            jax.ShapeDtypeStruct((held, own, PIX), f32),
        ]
        + [jax.ShapeDtypeStruct((items, own, PIX), bf)] * (groups - 1),
        compiler_params=params,
        cost_estimate=work(items, 2.1, 7.5),
        name="forward_items",
    )(my_group, *field_parts, perm, tin, inner_taps, vecs, item_vec)

    for s in range(1, groups):
        source = lax.rem(me + groups - s, groups) * items
        arrived = swap(sends[s - 1], "grp", s)
        block_out = lax.dynamic_update_slice(block_out, arrived.astype(f32), (source, 0, 0))

    pc = pd = mid_grad = None
    mid_vecs = 0.0
    item_grads = []
    for h in range(halves):
        start = h * some
        chained = h > 0
        cot = [cotangent] + cot_parts[h]
        extra = [pc, pd, mid_grad] if chained else []
        any_spec = pl.BlockSpec(memory_space=pl.ANY)

        def after(i):
            return jnp.minimum(i + 1, some - 1)

        def cot_specs(index, start=start):
            return [mine((own, PIX), 1, lambda i: index(i) + start)] + [
                pl.BlockSpec((1, own, PIX), lambda i, g: (index(i), 0, 0))
            ] * (groups - 1)

        pc, pd, mid_grad, dvec, ditem = pl.pallas_call(
            functools.partial(first_back_kernel, groups, some, chained),
            grid_spec=pltpu.PrefetchScalarGridSpec(
                num_scalar_prefetch=1,
                grid=(some,),
                in_specs=cot_specs(lambda i: 0)
                + cot_specs(after)
                + [
                    by_item((NJ, ROWS, C), 1, start),
                    by_item((2, 2 * C, ROWS), 1, start),
                    by_item((2, 2 * C, ROWS), 1, start),
                    by_item((8, C), 1, start),
                    by_item((8, C), 1, start),
                    whole((16, C)),
                    whole((2, TAPS, C, C)),
                ]
                + ([any_spec, any_spec, whole((2, TAPS * C, C))] if chained else []),
                out_specs=[
                    by_item(pad_shape, 1, start),
                    by_item(pad_shape, 1, start),
                    whole((2, TAPS * C, C)),
                    whole((8, C)),
                    by_item((8, C), 1),
                ],
                scratch_shapes=[
                    band,
                    tall,
                    pltpu.VMEM((NJ, ROWS, C), f32),
                    pltpu.VMEM((2, 3, 2 * C, 4 * C), f32),
                ],
            ),
            out_shape=[
                pads,
                pads,
                jax.ShapeDtypeStruct((2, TAPS * C, C), f32),
                jax.ShapeDtypeStruct((8, C), f32),
                jax.ShapeDtypeStruct((some, 8, C), f32),
            ],
            input_output_aliases={2 * groups + 8: 0, 2 * groups + 9: 1} if chained else {},
            compiler_params=params,
            cost_estimate=work(some, 3.1, 7.2),
            name="first_back_items",
        )(my_group, *cot, *cot, first_conv, x1t, x2t, stats, item_vec, vecs, inner_taps, *extra)
        mid_vecs = mid_vecs + dvec
        item_grads.append(ditem)
    ditem = jnp.concatenate(item_grads, axis=0)

    field_low, din, outer_vecs = pl.pallas_call(
        functools.partial(second_back_kernel, groups),
        grid=(items,),
        out_shape=[
            jax.ShapeDtypeStruct((groups, items, slots, cells), bf),
            jax.ShapeDtypeStruct((taps_rows, NJ * C), f32),
            jax.ShapeDtypeStruct((8, C), f32),
        ],
        in_specs=[
            by_item(pad_shape),
            by_item(pad_shape),
            by_item((NJ, ROWS, C)),
            by_item((taps_rows, ROWS)),
            by_item((8, C)),
            whole((16, C)),
            whole((taps_rows, NJ * C)),
            whole((8 * W, 8 * W)),
            whole((2, TAPS, C, C)),
        ],
        out_specs=[
            pl.BlockSpec((groups, 1, slots, cells), lambda i: (0, i, 0, 0)),
            whole((taps_rows, NJ * C)),
            whole((8, C)),
        ],
        scratch_shapes=[
            band,
            pltpu.VMEM((NJ, ROWS, C), f32),
            pltpu.VMEM((ROWS, NJ * C), bf),
        ],
        compiler_params=params,
        cost_estimate=work(items, 1.2, 4.6),
        name="second_back_items",
    )(pc, pd, lifted, im, stats, vecs, tin, perm, inner_taps)

    field_half = lax.all_to_all(field_low, "grp", split_axis=0, concat_axis=0, tiled=True)
    field_grad = field_half.reshape(held, slots, cells).astype(f32) * mask_float

    din = din.reshape(3, NJ + 2, slots, NJ, C)
    grad_in = sum(din[:, j : j + 3, :, j, :] for j in range(NJ)).reshape(TAPS * slots, C)
    time_grad = lax.dot_general(
        features,
        jnp.concatenate([ditem[:, 0, :], ditem[:, 1, :]], axis=1),
        (((0,), (0,)), ((), ())),
        precision=highest,
    )
    small = jnp.concatenate([time_grad.reshape(-1, C), mid_vecs], axis=0)
    count = small.shape[0]
    each = -(-count // devices)
    small = jnp.pad(small, ((0, each * devices - count), (0, 0))).reshape(devices, each, C)
    parts = jnp.concatenate([mid_grad.reshape(devices, share, C), small], axis=1)
    parts = lax.all_to_all(parts, both, split_axis=0, concat_axis=0, tiled=True)
    summed = jnp.sum(parts, axis=0)
    mid_total = summed[:share]
    spread = jnp.broadcast_to(summed[share:][None], (devices, each, C))
    spread = lax.all_to_all(spread, both, split_axis=0, concat_axis=0, tiled=True)
    spread = spread.reshape(devices * each, C)
    time_total = spread[: 2 * C].reshape(time_weight.shape)
    mid_vecs = spread[2 * C : 2 * C + 8]
    last = all_sum(jnp.concatenate([grad_in, outer_vecs], axis=0), both)
    in_total = last[: TAPS * slots]
    outer_vecs = last[TAPS * slots :]
    cot_row = mid_vecs[5:6]
    vec_total = jnp.concatenate(
        [outer_vecs[0:1] + cot_row, outer_vecs[1:3], mid_vecs[0:5], cot_row], axis=0
    )

    step_float = jnp.float32(STEP)
    in_new, in_first, in_second = adam_update(
        in_weight, in_total, in_moment, in_square, rate_in, step_float
    )
    mid_new, mid_first, mid_second = adam_update(
        mid_weight, mid_total, mid_moment, mid_square, rate_mid, step_float
    )
    time_new, time_first, time_second = adam_update(
        time_weight, time_total, time_moment, time_square, rate_time, step_float
    )
    vec_new, vec_first, vec_second = adam_update(
        vec_params, vec_total, vec_moment, vec_square, rate_vecs, step_float
    )
    return (
        block_out,
        field_grad,
        in_new,
        in_first,
        in_second,
        in_new.astype(bf),
        mid_new,
        mid_first,
        mid_second,
        mid_new.astype(bf),
        time_new,
        time_first,
        time_second,
        vec_new,
        vec_first,
        vec_second,
    )


def solution(mesh):
    rows = P(("wide", "grp"), None)
    return jax.shard_map(
        local,
        mesh=mesh,
        in_specs=(
            P("wide", None, "grp"),
            P("wide", None),
            P("wide"),
            P("wide", "grp", None),
            P(),
            P(),
            P(),
            rows,
            rows,
            rows,
            P(),
            P(),
            P(),
            P(),
            P(),
            P(),
        ),
        out_specs=(
            P("wide", "grp", None),
            P("wide", None, "grp"),
            P(),
            P(),
            P(),
            P(),
            rows,
            rows,
            rows,
            rows,
            P(),
            P(),
            P(),
            P(),
            P(),
            P(),
        ),
        check_vma=False,
    )
```

```python
import functools
import math

import jax
import jax.numpy as jnp
from jax import lax
from jax.experimental import pallas as pl
from jax.experimental.pallas import tpu as pltpu
from jax.sharding import PartitionSpec as P

C = 128
W = 64
H = 64
PIX = H * W
TAPS = 9
GROUPS = 8
STEP = 4
NJ = 4
NS = W // NJ
ROWS = H * NS

highest = lax.Precision.HIGHEST
beta_one = 0.5
beta_two = 0.5
epsilon = 1e-08
weight_decay = 0.01
rate_in = 0.1
rate_mid = 0.03
rate_time = 0.1
rate_vecs = 0.3
norm_epsilon = 1e-05
bf = jnp.bfloat16
f32 = jnp.float32
GELU_C = math.sqrt(2.0 / math.pi)
GELU_K = 0.044715
VMEM_LIMIT = 58 << 20


def fourier(noise_step, feature_count):
    half_count = feature_count // 2
    frequency = jnp.exp(-math.log(10000.0) * jnp.arange(half_count, dtype=jnp.float32) / half_count)
    angles = noise_step.astype(jnp.float32)[:, None] * frequency[None, :]
    return jnp.concatenate([jnp.sin(angles), jnp.cos(angles)], axis=1)


def adam_update(weight, grad, moment, square, rate, step_float):
    moment_new = beta_one * moment + (1.0 - beta_one) * grad
    square_new = beta_two * square + (1.0 - beta_two) * grad * grad
    moment_hat = moment_new / (1.0 - jnp.power(beta_one, step_float))
    square_hat = square_new / (1.0 - jnp.power(beta_two, step_float))
    weight_new = weight - rate * (
        moment_hat / (jnp.sqrt(square_hat) + epsilon) + weight_decay * weight
    )
    return (weight_new, moment_new, square_new)


def group_sum(v):
    lane = lax.broadcasted_iota(jnp.int32, v.shape, 1)
    for k in (1, 2, 4, 8):
        v = v + jnp.where((lane & k) == 0, pltpu.roll(v, C - k, 1), pltpu.roll(v, k, 1))
    return v


def rows8(v):
    return jnp.sum(v.reshape(v.shape[0] // 8, 8, v.shape[1]), axis=0)


def gelu_of_half(w):
    t = jnp.tanh(w * (2 * GELU_C + (8 * GELU_C * GELU_K) * (w * w)))
    return w + w * t


def slope_of_half(w):
    w2 = w * w
    t = jnp.tanh(w * (2 * GELU_C + (8 * GELU_C * GELU_K) * w2))
    v = w * (2 * GELU_C + (24 * GELU_C * GELU_K) * w2)
    return (1.0 + t) * (1.0 + (1.0 - t) * v)


def band_weights(k_ref, t_ref, adjoint):
    zero = jnp.zeros((C, C), bf)
    for a in range(3):
        for m in range(4):
            row = (a * 4 + m) * C
            for par in range(2):
                b = m - par
                if 0 <= b <= 2:
                    if adjoint:
                        block = k_ref[(2 - a) * 3 + (2 - b)].T * jnp.array(0.5, bf)
                    else:
                        block = k_ref[a * 3 + b]
                else:
                    block = zero
                t_ref[row : row + C, par * C : (par + 1) * C] = block


def put_padded(p_ref, j, v, y0, count):
    vb = v.astype(bf).reshape(count, NS, C)
    spots = [(j + 1, vb)]
    if j == NJ - 1:
        spots.append((0, pltpu.roll(v.reshape(count, NS, C), 1, 1).astype(bf)))
    if j == 0:
        spots.append((NJ + 1, pltpu.roll(v.reshape(count, NS, C), NS - 1, 1).astype(bf)))
    for slot, value in spots:
        p_ref[slot, pl.ds(y0 + 1, count)] = value
    return vb


def wrap_rows(p_ref):
    for slot in range(NJ + 2):
        p_ref[slot, 0] = p_ref[slot, H]
        p_ref[slot, H + 1] = p_ref[slot, 1]


def piece(p_ref, slot, a, y0, count):
    return p_ref[slot, pl.ds(a + y0, count)].reshape(count * NS, C)


def conv_rows(p_ref, t_ref, q, y0, count):
    left = jnp.concatenate(
        [piece(p_ref, 2 * q + m, a, y0, count) for a in range(3) for m in range(4)], axis=1
    )
    return jnp.dot(left, t_ref[...], preferred_element_type=f32)


def run(main, *others):
    main = list(main)
    rest = [step for other in others for step in other]
    done = 0
    for i, step in enumerate(main):
        step()
        upto = (i + 1) * len(rest) // len(main)
        for other in rest[done:upto]:
            other()
        done = upto


def weight_grad(xt_ref, at, p_ref, acc_ref, which):
    def step(a, n):
        total = None
        for q in range(2):
            right = jnp.concatenate(
                [piece(p_ref, 2 * q + 2 * n + m, a, 0, H) for m in range(2)], axis=1
            )
            part = jnp.dot(xt_ref[at, q], right, preferred_element_type=f32)
            total = part if total is None else total + part
        acc_ref[which, a, :, n * 2 * C : (n + 1) * 2 * C] += total

    return [functools.partial(step, a, n) for a in range(3) for n in range(2)]


def emit_weight_grad(acc_ref, which, out_ref):
    for a in range(3):
        for b in range(3):
            total = None
            for par in range(2):
                m = par + 2 - b
                block = acc_ref[which, 2 - a, par * C : (par + 1) * C, m * C : (m + 1) * C]
                total = block if total is None else total + block
            out_ref[which, (a * 3 + b) * C : (a * 3 + b + 1) * C, :] = total


def finish_stats(s1, s2, shift, alpha, bias, extra):
    inv = 1.0 / PIX
    s1 = jnp.sum(s1, axis=0, keepdims=True) * inv
    s2 = jnp.sum(s2, axis=0, keepdims=True) * inv
    mean = shift + s1
    var = jnp.maximum(s2 - s1 * s1, 0.0)
    mean_v = alpha * (mean + bias) + extra
    mu = group_sum(mean_v) * (1.0 / 16)
    centred = mean_v - mu
    group_var = group_sum(alpha * alpha * var + centred * centred) * (1.0 / 16)
    rstd = lax.rsqrt(group_var + norm_epsilon)
    return mean, var, mean_v, mu, rstd


def pick(index, options):
    chosen = options[0]
    for k in range(1, len(options)):
        chosen = jnp.where(index == k, options[k], chosen)
    return chosen


def chunks(count):
    return [(j, y0) for j in range(NJ) for y0 in range(0, H, count)]


def forward_kernel(
    groups,
    early_steps,
    me_ref,
    *refs,
):
    f_refs, refs = refs[:groups], refs[groups:]
    forward_items(groups, early_steps, me_ref[0], f_refs, *refs)


def forward_items(
    groups,
    early_steps,
    me,
    f_refs,
    perm_ref,
    tin_ref,
    k_ref,
    vec_ref,
    item_ref,
    lifted_ref,
    conv_ref,
    x1t_ref,
    x2t_ref,
    im_ref,
    stat_ref,
    *rest,
):
    own_ref, rest = rest[0], rest[1:]
    early_refs, late_refs, scratch = (
        rest[: groups - 1],
        rest[groups - 1 : (groups - 1) * 2],
        rest[(groups - 1) * 2 :],
    )
    is_early = pl.program_id(0) < early_steps
    t1_ref, t2_ref = scratch[:2]
    pads = (scratch[2:4], scratch[4:6])
    z_refs = scratch[6:8]
    own = C // groups

    @pl.when(pl.program_id(0) == 0)
    def _():
        band_weights(k_ref.at[0], t1_ref, False)
        band_weights(k_ref.at[1], t2_ref, False)

    def vec(i):
        return vec_ref[i : i + 1, :]

    def item(n):
        state = {}
        p1_ref, p2_ref = pads[n]
        z_ref = z_refs[n]

        def lift():
            parts = [ref[n].astype(f32) for ref in f_refs]
            raw = jnp.concatenate(
                [
                    pick(me, [parts[(g - k) % groups] for g in range(groups)])
                    for k in range(groups)
                ],
                axis=1,
            )
            rows = jnp.concatenate([raw[:, i * 512 : (i + 1) * 512] for i in range(8)], axis=0)
            spread = jnp.dot(rows.astype(bf), perm_ref[...], preferred_element_type=f32)
            lane = lax.broadcasted_iota(jnp.int32, (64, 128), 1) % NS
            cols = [spread[:, j * 128 : (j + 1) * 128] for j in range(NJ)]
            before = jnp.where(
                lane == 0, pltpu.roll(cols[3], 128 - 15, 1), pltpu.roll(cols[3], 1, 1)
            )
            after = jnp.where(
                lane == NS - 1, pltpu.roll(cols[0], 15, 1), pltpu.roll(cols[0], 127, 1)
            )
            taps = []
            for v in [before] + cols + [after]:
                taps.append(jnp.concatenate([v[i * 8 : (i + 1) * 8, :] for i in range(8)], axis=1))
            stack = jnp.concatenate(taps, axis=0)
            up = pltpu.roll(stack, NS, 1)
            down = pltpu.roll(stack, ROWS - NS, 1)
            im_ref[n] = jnp.concatenate([up, stack, down], axis=0).astype(bf)

        def clear():
            state["s1"] = jnp.zeros((8, C), f32)
            state["s2"] = jnp.zeros((8, C), f32)
            state["shift"] = None

        def gather_stats(x):
            if state["shift"] is None:
                state["shift"] = x[0:1, :]
            x = x - state["shift"]
            state["s1"] = state["s1"] + rows8(x)
            state["s2"] = state["s2"] + rows8(x * x)

        def conv_in(part):
            if part == 0:
                clear()
            left = im_ref[n, :, part * 256 : (part + 1) * 256]
            r = lax.dot_general(
                left, tin_ref[...], (((0,), (0,)), ((), ())), preferred_element_type=f32
            )
            for j in range(NJ):
                x = r[:, j * C : (j + 1) * C]
                lifted_ref[n, j, part * 256 : (part + 1) * 256, :] = x.astype(bf)
                gather_stats(x)

        def first_stats():
            one = jnp.ones((1, C), f32)
            zero = jnp.zeros((1, C), f32)
            mean, var, mean_v, mu, rstd = finish_stats(
                state["s1"], state["s2"], state["shift"], one, vec(0), zero
            )
            scale = rstd * vec(1)
            state["scale"] = 0.5 * scale
            state["base"] = 0.5 * ((mean_v - mu - mean) * scale + vec(2))
            state["one"] = [mean, var, mu, rstd]

        def normal(src_ref, p_ref, xt_ref, count, j, y0):
            at = slice(y0 * NS, (y0 + count) * NS)
            x = src_ref[n, j, at, :].astype(f32)
            v = gelu_of_half(x * state["scale"] + state["base"])
            vb = put_padded(p_ref, j, v, y0, count)
            xt_ref[n, j // 2, (j % 2) * C : (j % 2 + 1) * C, at] = vb.reshape(count * NS, C).T

        def conv_one(q, y0, count):
            if q == 0 and y0 == 0:
                clear()
            r = conv_rows(p1_ref, t1_ref, q, y0, count)
            for par in range(2):
                x = r[:, par * C : (par + 1) * C]
                conv_ref[n, 2 * q + par, y0 * NS : (y0 + count) * NS, :] = x.astype(bf)
                gather_stats(x)

        def second_stats():
            alpha = item_ref[n, 0:1, :]
            extra = item_ref[n, 1:2, :]
            mean, var, mean_v, mu, rstd = finish_stats(
                state["s1"], state["s2"], state["shift"], alpha, vec(3), extra
            )
            scale = rstd * alpha * vec(6)
            state["scale"] = 0.5 * scale
            state["base"] = 0.5 * ((mean_v - mu) * rstd * vec(6) - mean * scale + vec(7))
            stat_ref[n] = jnp.concatenate(state["one"] + [mean, var, mu, rstd], axis=0)

        def conv_two(q, y0, count):
            r = conv_rows(p2_ref, t2_ref, q, y0, count)
            add = vec(0) + vec(8)
            for par in range(2):
                j = 2 * q + par
                at = slice(y0 * NS, (y0 + count) * NS)
                x = r[:, par * C : (par + 1) * C] + lifted_ref[n, j, at, :].astype(f32) + add
                z_ref[pl.ds(y0 * W + j, count * NS, stride=NJ), :] = x

        def flip(i):
            at = slice(i * 128, (i + 1) * 128)
            t = z_ref[at, :].T
            for s in range(groups):
                chans = [(g + s) % groups * own for g in range(groups)]
                piece = pick(me, [t[c : c + own, :] for c in chans])
                if s == 0:
                    own_ref[n, :, at] = piece
                    continue
                piece = piece.astype(bf)
                early_ref = early_refs[s - 1]
                early_ref[n, :, at] = jnp.where(is_early, piece, early_ref[n, :, at])
                late_refs[s - 1][n, :, at] = piece

        part = functools.partial
        small, big = 8, 16
        bands = [(q, y0) for q in range(2) for y0 in range(0, H, big)]
        return {
            "lift": [lift] + [part(conv_in, k) for k in range(4)] + [first_stats],
            "one": [part(normal, lifted_ref, p1_ref, x1t_ref, small, *c) for c in chunks(small)]
            + [part(wrap_rows, p1_ref)],
            "conv1": [part(conv_one, *b, big) for b in bands] + [second_stats],
            "two": [part(normal, conv_ref, p2_ref, x2t_ref, small, *c) for c in chunks(small)]
            + [part(wrap_rows, p2_ref)],
            "conv2": [part(conv_two, *b, big) for b in bands],
            "flip": [part(flip, i) for i in range(PIX // 128)],
        }

    a, b = item(0), item(1)
    run(a["lift"])
    run(a["one"])
    run(a["conv1"], b["lift"], b["one"])
    run(b["conv1"], a["two"])
    run(a["conv2"], b["two"])
    run(b["conv2"], a["flip"])
    run(b["flip"])


def first_back_kernel(groups, items, chained, me_ref, *refs):
    step = pl.program_id(0)
    me = me_ref[0]
    start_refs, refs = refs[:groups], refs[groups:]
    next_refs, refs = refs[:groups], refs[groups:]
    conv_ref, x1t_ref, x2t_ref, stat_ref, item_ref, vec_ref, k_ref = refs[:7]
    refs = refs[7:]
    if chained:
        before_ref, refs = refs[2], refs[3:]
    pc_ref, pd_ref, dk_ref, dvec_ref, ditem_ref, t2_ref, z_ref, d_ref, acc_ref = refs
    pc_ref, pd_ref = pc_ref.at[0], pd_ref.at[0]
    part = functools.partial
    small, big = 8, 16

    def flip(src_refs, i):
        at = slice(i * 128, (i + 1) * 128)
        parts = [ref[0, :, at] for ref in src_refs]
        t = jnp.concatenate(
            [pick(me, [parts[(g - k) % groups] for g in range(groups)]) for k in range(groups)],
            axis=0,
        )
        z_ref[at, :] = t.astype(f32).T

    @pl.when(step == 0)
    def _():
        band_weights(k_ref.at[1], t2_ref, True)
        acc_ref[...] = jnp.zeros_like(acc_ref)
        dvec_ref[...] = jnp.zeros_like(dvec_ref)
        run([part(flip, start_refs, i) for i in range(PIX // 128)])

    def vec(i):
        return vec_ref[i : i + 1, :]

    def stat(i):
        return stat_ref[0, i : i + 1, :]

    cot_sum = jnp.zeros((8, C), f32)
    for j, y0 in chunks(big):
        v = z_ref[pl.ds(y0 * W + j, big * NS, stride=NJ), :]
        cot_sum = cot_sum + rows8(v)
        put_padded(pc_ref, j, v, y0, big)
    cot_sum = jnp.sum(cot_sum, axis=0, keepdims=True)
    wrap_rows(pc_ref)

    alpha = item_ref[0, 0:1, :]
    extra = item_ref[0, 1:2, :]
    mean, var, mu, rstd = stat(4), stat(5), stat(6), stat(7)
    mean_v = alpha * (mean + vec(3)) + extra
    sb, sx, sg, mean_en, c1, c2, c3, total = norm_back(
        pc_ref, t2_ref, conv_ref, d_ref, mean, mean_v, mu, rstd, alpha, vec(6), vec(7)
    )
    d_scaling = (
        rstd * (vec(6) * sx - mean_en * (rstd * alpha * PIX) * var) + (mean + vec(3)) * total
    )
    ditem_ref[0] = jnp.concatenate([d_scaling, total, jnp.zeros((6, C), f32)], axis=0)
    zero = jnp.zeros((1, C), f32)
    dvec_ref[...] += jnp.concatenate(
        [alpha * total, d_scaling, total, sg, sb, cot_sum, zero, zero], axis=0
    )

    def spread(j, y0):
        at = slice(y0 * NS, (y0 + small) * NS)
        x = conv_ref[0, j, at, :].astype(f32)
        put_padded(pd_ref, j, d_ref[j, at, :] * c1 + (x * c3 + c2), y0, small)

    run(
        weight_grad(x2t_ref, 0, pc_ref, acc_ref, 1),
        [part(spread, *c) for c in chunks(small)],
    )
    wrap_rows(pd_ref)
    run(
        weight_grad(x1t_ref, 0, pd_ref, acc_ref, 0),
        [part(flip, next_refs, i) for i in range(PIX // 128)],
    )

    @pl.when(step == items - 1)
    def _():
        emit_weight_grad(acc_ref, 0, dk_ref)
        emit_weight_grad(acc_ref, 1, dk_ref)
        if chained:
            dk_ref[...] += before_ref[...]


def norm_back(p_ref, t_ref, src_ref, d_ref, mean, mean_v, mu, rstd, alpha, gain, beta):
    big = 8
    slope = rstd * alpha
    centre = (mean_v - mu) * rstd
    scale = slope * gain
    half_scale = 0.5 * scale
    half_base = 0.5 * (centre * gain + beta - mean * scale)
    sums = [jnp.zeros((8, C), f32), jnp.zeros((8, C), f32)]

    def conv(q, y0):
        r = conv_rows(p_ref, t_ref, q, y0, big)
        for par in range(2):
            j = 2 * q + par
            at = slice(y0 * NS, (y0 + big) * NS)
            x = src_ref[0, j, at, :].astype(f32)
            d = r[:, par * C : (par + 1) * C] * slope_of_half(x * half_scale + half_base)
            d_ref[j, at, :] = d
            sums[0] = sums[0] + rows8(d)
            sums[1] = sums[1] + rows8(d * x)

    run([functools.partial(conv, q, y0) for q in range(2) for y0 in range(0, H, big)])
    sb = jnp.sum(sums[0], axis=0, keepdims=True)
    sx = jnp.sum(sums[1], axis=0, keepdims=True) - mean * sb
    sg = slope * sx + centre * sb
    inv = 1.0 / (16 * PIX)
    mean_e = group_sum(gain * sb) * inv
    mean_en = group_sum(gain * sg) * inv
    c1 = slope * gain
    c3 = -slope * slope * mean_en
    c2 = -slope * (mean_e + mean_en * centre) - c3 * mean
    total = rstd * (gain * sb - PIX * mean_e - PIX * mean_en * centre)
    return sb, sx, sg, mean_en, c1, c2, c3, total


def second_back_kernel(
    groups,
    pc_ref,
    pd_ref,
    lifted_ref,
    im_ref,
    stat_ref,
    vec_ref,
    tin_ref,
    perm_ref,
    k_ref,
    field_ref,
    din_ref,
    dvec_ref,
    t1_ref,
    d_ref,
    low_ref,
):
    small = 8
    pc_ref, pd_ref = pc_ref.at[0], pd_ref.at[0]

    @pl.when(pl.program_id(0) == 0)
    def _():
        band_weights(k_ref.at[0], t1_ref, True)
        din_ref[...] = jnp.zeros_like(din_ref)
        dvec_ref[...] = jnp.zeros_like(dvec_ref)

    def vec(i):
        return vec_ref[i : i + 1, :]

    def stat(i):
        return stat_ref[0, i : i + 1, :]

    one = jnp.ones((1, C), f32)
    mean, mu, rstd = stat(0), stat(2), stat(3)
    sb, sx, sg, mean_en, c1, c2, c3, total = norm_back(
        pd_ref, t1_ref, lifted_ref, d_ref, mean, mean + vec(0), mu, rstd, one, vec(1), vec(2)
    )
    for j, y0 in chunks(small):
        at = slice(y0 * NS, (y0 + small) * NS)
        x = lifted_ref[0, j, at, :].astype(f32)
        g = pc_ref[j + 1, y0 + 1 : y0 + 1 + small].reshape(small * NS, C).astype(f32)
        low_ref[at, j * C : (j + 1) * C] = (g + (d_ref[j, at, :] * c1 + (x * c3 + c2))).astype(bf)
    dvec_ref[...] += jnp.concatenate([total, sg, sb, jnp.zeros((5, C), f32)], axis=0)

    din_ref[...] += jnp.dot(im_ref[0], low_ref[...], preferred_element_type=f32)
    back = lax.dot_general(
        tin_ref[...], low_ref[...], (((1,), (1,)), ((), ())), preferred_element_type=f32
    )
    stack = (
        pltpu.roll(back[0:48], ROWS - NS, 1) + back[48:96] + pltpu.roll(back[96:144], NS, 1)
    )
    lane = lax.broadcasted_iota(jnp.int32, (64, 128), 1) % NS

    def tall(jj):
        v = stack[jj * 8 : (jj + 1) * 8, :]
        return jnp.concatenate([v[:, i * 128 : (i + 1) * 128] for i in range(8)], axis=0)

    before, after = tall(0), tall(NJ + 1)
    before = jnp.where(lane == NS - 1, pltpu.roll(before, 15, 1), pltpu.roll(before, 127, 1))
    after = jnp.where(lane == 0, pltpu.roll(after, 128 - 15, 1), pltpu.roll(after, 1, 1))
    cols = [tall(j + 1) for j in range(NJ)]
    cols[3] = cols[3] + before
    cols[0] = cols[0] + after
    rows = jnp.concatenate(cols, axis=1).astype(bf)
    spread = lax.dot_general(
        rows, perm_ref[...], (((1,), (1,)), ((), ())), preferred_element_type=f32
    )
    natural = jnp.concatenate([spread[i * 8 : (i + 1) * 8, :] for i in range(8)], axis=1)
    cells = PIX // groups
    for g in range(groups):
        field_ref[g, 0] = natural[:, g * cells : (g + 1) * cells].astype(bf)


def whole(shape):
    return pl.BlockSpec(shape, lambda i, *_: (0,) * len(shape))


def by_item(shape, count=1, start=0):
    return pl.BlockSpec((count,) + shape, lambda i, *_: (i + start,) + (0,) * len(shape))


def swap(x, axis, hops):
    size = lax.axis_size(axis)
    return lax.ppermute(x, axis, [(i, (i + hops) % size) for i in range(size)])


def all_sum(x, axis, bit=1, end=None):
    size = lax.axis_size(axis)
    end = size if end is None else end
    while bit < end:
        x = x + lax.ppermute(x, axis, [(i, i ^ bit) for i in range(size)])
        bit *= 2
    return x


def local(
    fields,
    slot_mask,
    noise_step,
    cotangent,
    in_weight,
    in_moment,
    in_square,
    mid_weight,
    mid_moment,
    mid_square,
    time_weight,
    time_moment,
    time_square,
    vec_params,
    vec_moment,
    vec_square,
):
    both = ("wide", "grp")
    groups = lax.axis_size("grp")
    devices = groups * lax.axis_size("wide")
    held = fields.shape[0]
    items = held // groups
    slots = fields.shape[1]
    own = cotangent.shape[1]
    cells = fields.shape[2]
    me = lax.axis_index("grp")
    first_item = me * items
    pair = 2
    halves = 2
    some = items // halves

    mask_float = slot_mask.astype(f32)[:, :, None]
    masked_low = (fields * mask_float).astype(bf)

    def to_peer(x, hops, start, count, after=None):
        at = lax.rem(me + hops, groups) * items + start
        part = lax.dynamic_slice_in_dim(x, at, count, 0)
        if after is not None:
            part, _ = lax.optimization_barrier((part, after))
        return swap(part, "grp", hops)

    field_parts = [masked_low] + [to_peer(masked_low, s, 0, items) for s in range(1, groups)]
    share = mid_weight.shape[0]
    copies = jnp.broadcast_to(mid_weight.astype(bf)[None], (devices, share, C))
    gathered = lax.all_to_all(copies, both, split_axis=0, concat_axis=0, tiled=True)
    inner_taps = gathered.reshape(2, TAPS, C, C)
    cot_parts = [
        [
            to_peer(cotangent, s, h * some, some, field_parts[-1] if h > 0 else None)
            for s in range(1, groups)
        ]
        for h in range(halves)
    ]

    taps_in = in_weight.astype(bf).reshape(3, 3, slots, C)
    tin = jnp.stack(
        [jnp.pad(taps_in, ((0, 0), (j, NJ - 1 - j), (0, 0), (0, 0))) for j in range(NJ)], axis=3
    ).reshape(3 * (NJ + 2) * slots, NJ * C)
    spot = jnp.arange(8 * W)
    goal = (spot % NJ) * 128 + (spot // W) * NS + (spot % W) // NJ
    perm = (goal[:, None] == spot[None, :]).astype(bf)

    steps = lax.dynamic_slice_in_dim(noise_step, first_item, items, 0)
    features = fourier(steps, time_weight.shape[0])
    scaling = jnp.dot(features, time_weight[:, :C], precision=highest) + vec_params[4][None, :]
    offset = jnp.dot(features, time_weight[:, C:], precision=highest) + vec_params[5][None, :]
    item_vec = jnp.stack([1.0 + scaling, offset] + [jnp.zeros_like(offset)] * 6, axis=1)
    vecs = jnp.pad(vec_params, ((0, 7), (0, 0)))

    act = jax.ShapeDtypeStruct((items, NJ, ROWS, C), bf)
    flat = jax.ShapeDtypeStruct((items, 2, 2 * C, ROWS), bf)
    taps_rows = 3 * (NJ + 2) * slots
    pad_shape = (NJ + 2, H + 2, NS, C)
    pads = jax.ShapeDtypeStruct((items,) + pad_shape, bf)
    row = jax.ShapeDtypeStruct((items, 8, C), f32)
    band = pltpu.VMEM((12 * C, 2 * C), bf)
    tall = pltpu.VMEM((PIX, C), f32)
    params = pltpu.CompilerParams(vmem_limit_bytes=VMEM_LIMIT)
    my_group = me.astype(jnp.int32).reshape(1)

    def work(count, size, moved):
        gain = 2 * TAPS * C * C * PIX
        return pl.CostEstimate(
            flops=int(count * size * gain * 2),
            bytes_accessed=int(count * moved * 2 * C * PIX),
            transcendentals=0,
        )

    def mine(shape, count, index):
        return pl.BlockSpec(
            (count,) + shape, lambda i, g: (g[0] * (items // count) + index(i), 0, 0)
        )

    steps = items // pair
    early_steps = max(1, steps // 2)
    late_steps = max(1, steps - early_steps)
    early = early_steps * pair
    lifted, first_conv, x1t, x2t, im, stats, block_out, *sends = pl.pallas_call(
        functools.partial(forward_kernel, groups, early_steps),
        grid_spec=pltpu.PrefetchScalarGridSpec(
            num_scalar_prefetch=1,
            grid=(items // pair,),
            in_specs=[mine((slots, cells), pair, lambda i: i)]
            + [by_item((slots, cells), pair)] * (groups - 1)
            + [
                whole((8 * W, 8 * W)),
                whole((taps_rows, NJ * C)),
                whole((2, TAPS, C, C)),
                whole((16, C)),
                by_item((8, C), pair),
            ],
            out_specs=[
                by_item((NJ, ROWS, C), pair),
                by_item((NJ, ROWS, C), pair),
                by_item((2, 2 * C, ROWS), pair),
                by_item((2, 2 * C, ROWS), pair),
                by_item((taps_rows, ROWS), pair),
                by_item((8, C), pair),
                mine((own, PIX), pair, lambda i: i),
            ]
            + [
                pl.BlockSpec(
                    (pair, own, PIX), lambda i, g: (jnp.minimum(i, early_steps - 1), 0, 0)
                )
            ]
            * (groups - 1)
            + [
                pl.BlockSpec(
                    (pair, own, PIX), lambda i, g: (jnp.maximum(i - early_steps, 0), 0, 0)
                )
            ]
            * (groups - 1),
            scratch_shapes=[band] * 2 + [pltpu.VMEM(pad_shape, bf)] * 4 + [tall] * 2,
        ),
        out_shape=[
            act,
            act,
            flat,
            flat,
            jax.ShapeDtypeStruct((items, taps_rows, ROWS), bf),
            row,
            jax.ShapeDtypeStruct((held, own, PIX), f32),
        ]
        + [jax.ShapeDtypeStruct((early, own, PIX), bf)] * (groups - 1)
        + [jax.ShapeDtypeStruct((late_steps * pair, own, PIX), bf)] * (groups - 1),
        compiler_params=params,
        cost_estimate=work(items, 2.1, 7.5),
        name="forward_items",
    )(my_group, *field_parts, perm, tin, inner_taps, vecs, item_vec)

    sent = [[swap(sends[s - 1], "grp", s) for s in range(1, groups)]]
    late = sends[groups - 1 :] if early < items else []
    sent.append([swap(x, "grp", s + 1) for s, x in enumerate(late)])

    pc = pd = mid_grad = None
    mid_vecs = 0.0
    item_grads = []
    for h in range(halves):
        start = h * some
        chained = h > 0
        cot = [cotangent] + cot_parts[h]
        extra = [pc, pd, mid_grad] if chained else []
        any_spec = pl.BlockSpec(memory_space=pl.ANY)

        def after(i):
            return jnp.minimum(i + 1, some - 1)

        def cot_specs(index, start=start):
            return [mine((own, PIX), 1, lambda i: index(i) + start)] + [
                pl.BlockSpec((1, own, PIX), lambda i, g: (index(i), 0, 0))
            ] * (groups - 1)

        pc, pd, mid_grad, dvec, ditem = pl.pallas_call(
            functools.partial(first_back_kernel, groups, some, chained),
            grid_spec=pltpu.PrefetchScalarGridSpec(
                num_scalar_prefetch=1,
                grid=(some,),
                in_specs=cot_specs(lambda i: 0)
                + cot_specs(after)
                + [
                    by_item((NJ, ROWS, C), 1, start),
                    by_item((2, 2 * C, ROWS), 1, start),
                    by_item((2, 2 * C, ROWS), 1, start),
                    by_item((8, C), 1, start),
                    by_item((8, C), 1, start),
                    whole((16, C)),
                    whole((2, TAPS, C, C)),
                ]
                + ([any_spec, any_spec, whole((2, TAPS * C, C))] if chained else []),
                out_specs=[
                    by_item(pad_shape, 1, start),
                    by_item(pad_shape, 1, start),
                    whole((2, TAPS * C, C)),
                    whole((8, C)),
                    by_item((8, C), 1),
                ],
                scratch_shapes=[
                    band,
                    tall,
                    pltpu.VMEM((NJ, ROWS, C), f32),
                    pltpu.VMEM((2, 3, 2 * C, 4 * C), f32),
                ],
            ),
            out_shape=[
                pads,
                pads,
                jax.ShapeDtypeStruct((2, TAPS * C, C), f32),
                jax.ShapeDtypeStruct((8, C), f32),
                jax.ShapeDtypeStruct((some, 8, C), f32),
            ],
            input_output_aliases={2 * groups + 8: 0, 2 * groups + 9: 1} if chained else {},
            compiler_params=params,
            cost_estimate=work(some, 3.1, 7.2),
            name="first_back_items",
        )(my_group, *cot, *cot, first_conv, x1t, x2t, stats, item_vec, vecs, inner_taps, *extra)
        mid_vecs = mid_vecs + dvec
        item_grads.append(ditem)
    ditem = jnp.concatenate(item_grads, axis=0)

    wide = lax.axis_size("wide")
    small = jnp.concatenate([features, ditem[:, 0, :], ditem[:, 1, :], mid_vecs], axis=0)
    small = jnp.broadcast_to(small[None], (wide,) + small.shape)
    shares = groups * share
    parts = jnp.concatenate([mid_grad.reshape(wide, shares, C), small], axis=1)
    parts = lax.all_to_all(parts, "wide", split_axis=0, concat_axis=0, tiled=True)

    stats, sent[0] = lax.optimization_barrier((stats, sent[0]))
    field_low, din, outer_vecs = pl.pallas_call(
        functools.partial(second_back_kernel, groups),
        grid=(items,),
        out_shape=[
            jax.ShapeDtypeStruct((groups, items, slots, cells), bf),
            jax.ShapeDtypeStruct((taps_rows, NJ * C), f32),
            jax.ShapeDtypeStruct((8, C), f32),
        ],
        in_specs=[
            by_item(pad_shape),
            by_item(pad_shape),
            by_item((NJ, ROWS, C)),
            by_item((taps_rows, ROWS)),
            by_item((8, C)),
            whole((16, C)),
            whole((taps_rows, NJ * C)),
            whole((8 * W, 8 * W)),
            whole((2, TAPS, C, C)),
        ],
        out_specs=[
            pl.BlockSpec((groups, 1, slots, cells), lambda i: (0, i, 0, 0)),
            whole((taps_rows, NJ * C)),
            whole((8, C)),
        ],
        scratch_shapes=[
            band,
            pltpu.VMEM((NJ, ROWS, C), f32),
            pltpu.VMEM((ROWS, NJ * C), bf),
        ],
        compiler_params=params,
        cost_estimate=work(items, 1.2, 4.6),
        name="second_back_items",
    )(pc, pd, lifted, im, stats, vecs, tin, perm, inner_taps)

    din, parts = lax.optimization_barrier((din, parts))
    din = din.reshape(3, NJ + 2, slots, NJ, C)
    grad_in = sum(din[:, j : j + 3, :, j, :] for j in range(NJ)).reshape(TAPS * slots, C)
    small = parts[:, shares:]
    all_features = small[:, :items].reshape(wide * items, C)
    time_rows = [
        lax.dot_general(
            all_features,
            small[:, k * items : (k + 1) * items].reshape(wide * items, C),
            (((0,), (0,)), ((), ())),
            precision=highest,
        )
        for k in (1, 2)
    ]
    rows_all = jnp.concatenate(time_rows + [jnp.sum(small[:, 3 * items :], axis=0)], axis=0)
    partial = jnp.sum(parts[:, :shares], axis=0)
    last = all_sum(jnp.concatenate([grad_in, outer_vecs], axis=0), "wide", 1, 2)
    last, field_low, sent[0] = lax.optimization_barrier((last, field_low, sent[0]))
    field_grad = jnp.zeros((held, slots, cells), f32)
    for s in range(groups):
        source = lax.rem(me + groups - s, groups) * items
        block = lax.dynamic_index_in_dim(field_low, lax.rem(me + s, groups), 0, False)
        if s > 0:
            block = swap(block, "grp", s)
        field_grad = lax.dynamic_update_slice(field_grad, block.astype(f32), (source, 0, 0))
    field_grad = field_grad * mask_float

    last = all_sum(last, "wide", 2)
    rows_in = last.shape[0]
    last, sent[1] = lax.optimization_barrier((last, sent[1]))
    for start, arrived in ((0, sent[0]), (early, sent[1])):
        for s, block in enumerate(arrived):
            source = lax.rem(me + groups - s - 1, groups) * items
            block_out = lax.dynamic_update_slice(
                block_out, block.astype(f32), (source + start, 0, 0)
            )
    last = all_sum(jnp.concatenate([last, rows_all, partial], axis=0), "grp")
    rows_all = last[rows_in : rows_in + rows_all.shape[0]]
    time_total = jnp.concatenate([rows_all[:C], rows_all[C : 2 * C]], axis=1)
    mid_vecs = rows_all[2 * C :]
    partial = last[last.shape[0] - shares :].reshape(groups, share, C)
    mid_total = lax.dynamic_index_in_dim(partial, me, 0, False)
    last = last[:rows_in]
    in_total = last[: TAPS * slots]
    outer_vecs = last[TAPS * slots :]
    cot_row = mid_vecs[5:6]
    vec_total = jnp.concatenate(
        [outer_vecs[0:1] + cot_row, outer_vecs[1:3], mid_vecs[0:5], cot_row], axis=0
    )

    step_float = jnp.float32(STEP)
    in_new, in_first, in_second = adam_update(
        in_weight, in_total, in_moment, in_square, rate_in, step_float
    )
    mid_new, mid_first, mid_second = adam_update(
        mid_weight, mid_total, mid_moment, mid_square, rate_mid, step_float
    )
    time_new, time_first, time_second = adam_update(
        time_weight, time_total, time_moment, time_square, rate_time, step_float
    )
    vec_new, vec_first, vec_second = adam_update(
        vec_params, vec_total, vec_moment, vec_square, rate_vecs, step_float
    )
    return (
        block_out,
        field_grad,
        in_new,
        in_first,
        in_second,
        in_new.astype(bf),
        mid_new,
        mid_first,
        mid_second,
        mid_new.astype(bf),
        time_new,
        time_first,
        time_second,
        vec_new,
        vec_first,
        vec_second,
    )


def solution(mesh):
    rows = P(("wide", "grp"), None)
    return jax.shard_map(
        local,
        mesh=mesh,
        in_specs=(
            P("wide", None, "grp"),
            P("wide", None),
            P("wide"),
            P("wide", "grp", None),
            P(),
            P(),
            P(),
            rows,
            rows,
            rows,
            P(),
            P(),
            P(),
            P(),
            P(),
            P(),
        ),
        out_specs=(
            P("wide", "grp", None),
            P("wide", None, "grp"),
            P(),
            P(),
            P(),
            P(),
            rows,
            rows,
            rows,
            rows,
            P(),
            P(),
            P(),
            P(),
            P(),
            P(),
        ),
        check_vma=False,
    )
```

```python
import functools
import math

import jax
import jax.numpy as jnp
from jax import lax
from jax.experimental import pallas as pl
from jax.experimental.pallas import tpu as pltpu
from jax.sharding import PartitionSpec as P

C = 128
W = 64
H = 64
PIX = H * W
TAPS = 9
GROUPS = 8
STEP = 4
NJ = 4
NS = W // NJ
ROWS = H * NS

highest = lax.Precision.HIGHEST
beta_one = 0.5
beta_two = 0.5
epsilon = 1e-08
weight_decay = 0.01
rate_in = 0.1
rate_mid = 0.03
rate_time = 0.1
rate_vecs = 0.3
norm_epsilon = 1e-05
bf = jnp.bfloat16
f32 = jnp.float32
GELU_C = math.sqrt(2.0 / math.pi)
GELU_K = 0.044715
VMEM_LIMIT = 58 << 20


def fourier(noise_step, feature_count):
    half_count = feature_count // 2
    frequency = jnp.exp(-math.log(10000.0) * jnp.arange(half_count, dtype=jnp.float32) / half_count)
    angles = noise_step.astype(jnp.float32)[:, None] * frequency[None, :]
    return jnp.concatenate([jnp.sin(angles), jnp.cos(angles)], axis=1)


def adam_update(weight, grad, moment, square, rate, step_float):
    moment_new = beta_one * moment + (1.0 - beta_one) * grad
    square_new = beta_two * square + (1.0 - beta_two) * grad * grad
    moment_hat = moment_new / (1.0 - jnp.power(beta_one, step_float))
    square_hat = square_new / (1.0 - jnp.power(beta_two, step_float))
    weight_new = weight - rate * (
        moment_hat / (jnp.sqrt(square_hat) + epsilon) + weight_decay * weight
    )
    return (weight_new, moment_new, square_new)


def group_sum(v):
    lane = lax.broadcasted_iota(jnp.int32, v.shape, 1)
    for k in (1, 2, 4, 8):
        v = v + jnp.where((lane & k) == 0, pltpu.roll(v, C - k, 1), pltpu.roll(v, k, 1))
    return v


def rows8(v):
    return jnp.sum(v.reshape(v.shape[0] // 8, 8, v.shape[1]), axis=0)


def gelu_of_half(w):
    t = jnp.tanh(w * (2 * GELU_C + (8 * GELU_C * GELU_K) * (w * w)))
    return w + w * t


def slope_of_half(w):
    w2 = w * w
    t = jnp.tanh(w * (2 * GELU_C + (8 * GELU_C * GELU_K) * w2))
    v = w * (2 * GELU_C + (24 * GELU_C * GELU_K) * w2)
    return (1.0 + t) * (1.0 + (1.0 - t) * v)


def band_weights(k_ref, t_ref, adjoint):
    zero = jnp.zeros((C, C), bf)
    for a in range(3):
        for m in range(4):
            row = (a * 4 + m) * C
            for par in range(2):
                b = m - par
                if 0 <= b <= 2:
                    if adjoint:
                        block = k_ref[(2 - a) * 3 + (2 - b)].T * jnp.array(0.5, bf)
                    else:
                        block = k_ref[a * 3 + b]
                else:
                    block = zero
                t_ref[row : row + C, par * C : (par + 1) * C] = block


def put_padded(p_ref, j, v, y0, count):
    vb = v.astype(bf).reshape(count, NS, C)
    spots = [(j + 1, vb)]
    if j == NJ - 1:
        spots.append((0, pltpu.roll(v.reshape(count, NS, C), 1, 1).astype(bf)))
    if j == 0:
        spots.append((NJ + 1, pltpu.roll(v.reshape(count, NS, C), NS - 1, 1).astype(bf)))
    for slot, value in spots:
        p_ref[slot, pl.ds(y0 + 1, count)] = value
    return vb


def wrap_rows(p_ref):
    for slot in range(NJ + 2):
        p_ref[slot, 0] = p_ref[slot, H]
        p_ref[slot, H + 1] = p_ref[slot, 1]


def piece(p_ref, slot, a, y0, count):
    return p_ref[slot, pl.ds(a + y0, count)].reshape(count * NS, C)


def conv_rows(p_ref, t_ref, q, y0, count):
    left = jnp.concatenate(
        [piece(p_ref, 2 * q + m, a, y0, count) for a in range(3) for m in range(4)], axis=1
    )
    return jnp.dot(left, t_ref[...], preferred_element_type=f32)


def run(main, *others):
    main = list(main)
    rest = [step for other in others for step in other]
    done = 0
    for i, step in enumerate(main):
        step()
        upto = (i + 1) * len(rest) // len(main)
        for other in rest[done:upto]:
            other()
        done = upto


def weight_grad(xt_ref, at, p_ref, acc_ref, which):
    def step(a, n):
        total = None
        for q in range(2):
            right = jnp.concatenate(
                [piece(p_ref, 2 * q + 2 * n + m, a, 0, H) for m in range(2)], axis=1
            )
            part = jnp.dot(xt_ref[at, q], right, preferred_element_type=f32)
            total = part if total is None else total + part
        acc_ref[which, a, :, n * 2 * C : (n + 1) * 2 * C] += total

    return [functools.partial(step, a, n) for a in range(3) for n in range(2)]


def emit_weight_grad(acc_ref, which, out_ref):
    for a in range(3):
        for b in range(3):
            total = None
            for par in range(2):
                m = par + 2 - b
                block = acc_ref[which, 2 - a, par * C : (par + 1) * C, m * C : (m + 1) * C]
                total = block if total is None else total + block
            out_ref[which, (a * 3 + b) * C : (a * 3 + b + 1) * C, :] = total


def finish_stats(s1, s2, shift, alpha, bias, extra):
    inv = 1.0 / PIX
    s1 = jnp.sum(s1, axis=0, keepdims=True) * inv
    s2 = jnp.sum(s2, axis=0, keepdims=True) * inv
    mean = shift + s1
    var = jnp.maximum(s2 - s1 * s1, 0.0)
    mean_v = alpha * (mean + bias) + extra
    mu = group_sum(mean_v) * (1.0 / 16)
    centred = mean_v - mu
    group_var = group_sum(alpha * alpha * var + centred * centred) * (1.0 / 16)
    rstd = lax.rsqrt(group_var + norm_epsilon)
    return mean, var, mean_v, mu, rstd


def pick(index, options):
    chosen = options[0]
    for k in range(1, len(options)):
        chosen = jnp.where(index == k, options[k], chosen)
    return chosen


def chunks(count):
    return [(j, y0) for j in range(NJ) for y0 in range(0, H, count)]


def forward_kernel(
    groups,
    early_steps,
    me_ref,
    *refs,
):
    f_refs, refs = refs[:groups], refs[groups:]
    forward_items(groups, early_steps, me_ref[0], f_refs, *refs)


def forward_items(
    groups,
    early_steps,
    me,
    f_refs,
    perm_ref,
    tin_ref,
    k_ref,
    vec_ref,
    item_ref,
    lifted_ref,
    conv_ref,
    x1t_ref,
    x2t_ref,
    im_ref,
    stat_ref,
    *rest,
):
    own_ref, rest = rest[0], rest[1:]
    early_refs, late_refs, scratch = (
        rest[: groups - 1],
        rest[groups - 1 : (groups - 1) * 2],
        rest[(groups - 1) * 2 :],
    )
    is_early = pl.program_id(0) < early_steps
    t1_ref, t2_ref = scratch[:2]
    pads = (scratch[2:4], scratch[4:6])
    z_refs = scratch[6:8]
    own = C // groups

    @pl.when(pl.program_id(0) == 0)
    def _():
        band_weights(k_ref.at[0], t1_ref, False)
        band_weights(k_ref.at[1], t2_ref, False)

    def vec(i):
        return vec_ref[i : i + 1, :]

    def item(n):
        state = {}
        p1_ref, p2_ref = pads[n]
        z_ref = z_refs[n]

        def lift():
            parts = [ref[n].astype(f32) for ref in f_refs]
            raw = jnp.concatenate(
                [
                    pick(me, [parts[(g - k) % groups] for g in range(groups)])
                    for k in range(groups)
                ],
                axis=1,
            )
            rows = jnp.concatenate([raw[:, i * 512 : (i + 1) * 512] for i in range(8)], axis=0)
            spread = jnp.dot(rows.astype(bf), perm_ref[...], preferred_element_type=f32)
            lane = lax.broadcasted_iota(jnp.int32, (64, 128), 1) % NS
            cols = [spread[:, j * 128 : (j + 1) * 128] for j in range(NJ)]
            before = jnp.where(
                lane == 0, pltpu.roll(cols[3], 128 - 15, 1), pltpu.roll(cols[3], 1, 1)
            )
            after = jnp.where(
                lane == NS - 1, pltpu.roll(cols[0], 15, 1), pltpu.roll(cols[0], 127, 1)
            )
            taps = []
            for v in [before] + cols + [after]:
                taps.append(jnp.concatenate([v[i * 8 : (i + 1) * 8, :] for i in range(8)], axis=1))
            stack = jnp.concatenate(taps, axis=0)
            up = pltpu.roll(stack, NS, 1)
            down = pltpu.roll(stack, ROWS - NS, 1)
            im_ref[n] = jnp.concatenate([up, stack, down], axis=0).astype(bf)

        def clear():
            state["s1"] = jnp.zeros((8, C), f32)
            state["s2"] = jnp.zeros((8, C), f32)
            state["shift"] = None

        def gather_stats(x):
            if state["shift"] is None:
                state["shift"] = x[0:1, :]
            x = x - state["shift"]
            state["s1"] = state["s1"] + rows8(x)
            state["s2"] = state["s2"] + rows8(x * x)

        def conv_in(part):
            if part == 0:
                clear()
            left = im_ref[n, :, part * 256 : (part + 1) * 256]
            r = lax.dot_general(
                left, tin_ref[...], (((0,), (0,)), ((), ())), preferred_element_type=f32
            )
            for j in range(NJ):
                x = r[:, j * C : (j + 1) * C]
                lifted_ref[n, j, part * 256 : (part + 1) * 256, :] = x.astype(bf)
                gather_stats(x)

        def first_stats():
            one = jnp.ones((1, C), f32)
            zero = jnp.zeros((1, C), f32)
            mean, var, mean_v, mu, rstd = finish_stats(
                state["s1"], state["s2"], state["shift"], one, vec(0), zero
            )
            scale = rstd * vec(1)
            state["scale"] = 0.5 * scale
            state["base"] = 0.5 * ((mean_v - mu - mean) * scale + vec(2))
            state["one"] = [mean, var, mu, rstd]

        def normal(src_ref, p_ref, xt_ref, count, j, y0):
            at = slice(y0 * NS, (y0 + count) * NS)
            x = src_ref[n, j, at, :].astype(f32)
            v = gelu_of_half(x * state["scale"] + state["base"])
            vb = put_padded(p_ref, j, v, y0, count)
            xt_ref[n, j // 2, (j % 2) * C : (j % 2 + 1) * C, at] = vb.reshape(count * NS, C).T

        def conv_one(q, y0, count):
            if q == 0 and y0 == 0:
                clear()
            r = conv_rows(p1_ref, t1_ref, q, y0, count)
            for par in range(2):
                x = r[:, par * C : (par + 1) * C]
                conv_ref[n, 2 * q + par, y0 * NS : (y0 + count) * NS, :] = x.astype(bf)
                gather_stats(x)

        def second_stats():
            alpha = item_ref[n, 0:1, :]
            extra = item_ref[n, 1:2, :]
            mean, var, mean_v, mu, rstd = finish_stats(
                state["s1"], state["s2"], state["shift"], alpha, vec(3), extra
            )
            scale = rstd * alpha * vec(6)
            state["scale"] = 0.5 * scale
            state["base"] = 0.5 * ((mean_v - mu) * rstd * vec(6) - mean * scale + vec(7))
            stat_ref[n] = jnp.concatenate(state["one"] + [mean, var, mu, rstd], axis=0)

        def conv_two(q, y0, count):
            r = conv_rows(p2_ref, t2_ref, q, y0, count)
            add = vec(0) + vec(8)
            for par in range(2):
                j = 2 * q + par
                at = slice(y0 * NS, (y0 + count) * NS)
                x = r[:, par * C : (par + 1) * C] + lifted_ref[n, j, at, :].astype(f32) + add
                z_ref[pl.ds(y0 * W + j, count * NS, stride=NJ), :] = x

        def flip(i):
            at = slice(i * 128, (i + 1) * 128)
            t = z_ref[at, :].T
            for s in range(groups):
                chans = [(g + s) % groups * own for g in range(groups)]
                piece = pick(me, [t[c : c + own, :] for c in chans])
                if s == 0:
                    own_ref[n, :, at] = piece
                    continue
                piece = piece.astype(bf)
                early_ref = early_refs[s - 1]
                early_ref[n, :, at] = jnp.where(is_early, piece, early_ref[n, :, at])
                late_refs[s - 1][n, :, at] = piece

        part = functools.partial
        small, big = 8, 16
        bands = [(q, y0) for q in range(2) for y0 in range(0, H, big)]
        return {
            "lift": [lift] + [part(conv_in, k) for k in range(4)] + [first_stats],
            "one": [part(normal, lifted_ref, p1_ref, x1t_ref, small, *c) for c in chunks(small)]
            + [part(wrap_rows, p1_ref)],
            "conv1": [part(conv_one, *b, big) for b in bands] + [second_stats],
            "two": [part(normal, conv_ref, p2_ref, x2t_ref, small, *c) for c in chunks(small)]
            + [part(wrap_rows, p2_ref)],
            "conv2": [part(conv_two, *b, big) for b in bands],
            "flip": [part(flip, i) for i in range(PIX // 128)],
        }

    a, b = item(0), item(1)
    run(a["lift"])
    run(a["one"])
    run(a["conv1"], b["lift"], b["one"])
    run(b["conv1"], a["two"])
    run(a["conv2"], b["two"])
    run(b["conv2"], a["flip"])
    run(b["flip"])


def first_back_kernel(groups, items, chained, me_ref, *refs):
    step = pl.program_id(0)
    me = me_ref[0]
    start_refs, refs = refs[:groups], refs[groups:]
    next_refs, refs = refs[:groups], refs[groups:]
    conv_ref, x1t_ref, x2t_ref, stat_ref, item_ref, vec_ref, k_ref = refs[:7]
    refs = refs[7:]
    if chained:
        before_ref, refs = refs[2], refs[3:]
    pc_ref, pd_ref, dk_ref, dvec_ref, ditem_ref, t2_ref, z_ref, d_ref, acc_ref = refs
    pc_ref, pd_ref = pc_ref.at[0], pd_ref.at[0]
    part = functools.partial
    small, big = 8, 16

    def flip(src_refs, i):
        at = slice(i * 128, (i + 1) * 128)
        parts = [ref[0, :, at] for ref in src_refs]
        t = jnp.concatenate(
            [pick(me, [parts[(g - k) % groups] for g in range(groups)]) for k in range(groups)],
            axis=0,
        )
        z_ref[at, :] = t.astype(f32).T

    @pl.when(step == 0)
    def _():
        band_weights(k_ref.at[1], t2_ref, True)
        acc_ref[...] = jnp.zeros_like(acc_ref)
        dvec_ref[...] = jnp.zeros_like(dvec_ref)
        run([part(flip, start_refs, i) for i in range(PIX // 128)])

    def vec(i):
        return vec_ref[i : i + 1, :]

    def stat(i):
        return stat_ref[0, i : i + 1, :]

    cot_sum = jnp.zeros((8, C), f32)
    for j, y0 in chunks(big):
        v = z_ref[pl.ds(y0 * W + j, big * NS, stride=NJ), :]
        cot_sum = cot_sum + rows8(v)
        put_padded(pc_ref, j, v, y0, big)
    cot_sum = jnp.sum(cot_sum, axis=0, keepdims=True)
    wrap_rows(pc_ref)

    alpha = item_ref[0, 0:1, :]
    extra = item_ref[0, 1:2, :]
    mean, var, mu, rstd = stat(4), stat(5), stat(6), stat(7)
    mean_v = alpha * (mean + vec(3)) + extra
    products = weight_grad(x2t_ref, 0, pc_ref, acc_ref, 1)
    sb, sx, sg, mean_en, c1, c2, c3, total = norm_back(
        pc_ref,
        t2_ref,
        conv_ref,
        d_ref,
        mean,
        mean_v,
        mu,
        rstd,
        alpha,
        vec(6),
        vec(7),
        products[:3],
    )
    d_scaling = (
        rstd * (vec(6) * sx - mean_en * (rstd * alpha * PIX) * var) + (mean + vec(3)) * total
    )
    ditem_ref[0] = jnp.concatenate([d_scaling, total, jnp.zeros((6, C), f32)], axis=0)
    zero = jnp.zeros((1, C), f32)
    dvec_ref[...] += jnp.concatenate(
        [alpha * total, d_scaling, total, sg, sb, cot_sum, zero, zero], axis=0
    )

    def spread(j, y0):
        at = slice(y0 * NS, (y0 + small) * NS)
        x = conv_ref[0, j, at, :].astype(f32)
        put_padded(pd_ref, j, d_ref[j, at, :] * c1 + (x * c3 + c2), y0, small)

    run(
        products[3:],
        [part(spread, *c) for c in chunks(small)],
    )
    wrap_rows(pd_ref)
    run(
        weight_grad(x1t_ref, 0, pd_ref, acc_ref, 0),
        [part(flip, next_refs, i) for i in range(PIX // 128)],
    )

    @pl.when(step == items - 1)
    def _():
        emit_weight_grad(acc_ref, 0, dk_ref)
        emit_weight_grad(acc_ref, 1, dk_ref)
        if chained:
            dk_ref[...] += before_ref[...]


def norm_back(p_ref, t_ref, src_ref, d_ref, mean, mean_v, mu, rstd, alpha, gain, beta, others=()):
    big = 8
    slope = rstd * alpha
    centre = (mean_v - mu) * rstd
    scale = slope * gain
    half_scale = 0.5 * scale
    half_base = 0.5 * (centre * gain + beta - mean * scale)
    sums = [jnp.zeros((8, C), f32), jnp.zeros((8, C), f32)]

    def conv(q, y0):
        r = conv_rows(p_ref, t_ref, q, y0, big)
        for par in range(2):
            j = 2 * q + par
            at = slice(y0 * NS, (y0 + big) * NS)
            x = src_ref[0, j, at, :].astype(f32)
            d = r[:, par * C : (par + 1) * C] * slope_of_half(x * half_scale + half_base)
            d_ref[j, at, :] = d
            sums[0] = sums[0] + rows8(d)
            sums[1] = sums[1] + rows8(d * x)

    run([functools.partial(conv, q, y0) for q in range(2) for y0 in range(0, H, big)], others)
    sb = jnp.sum(sums[0], axis=0, keepdims=True)
    sx = jnp.sum(sums[1], axis=0, keepdims=True) - mean * sb
    sg = slope * sx + centre * sb
    inv = 1.0 / (16 * PIX)
    mean_e = group_sum(gain * sb) * inv
    mean_en = group_sum(gain * sg) * inv
    c1 = slope * gain
    c3 = -slope * slope * mean_en
    c2 = -slope * (mean_e + mean_en * centre) - c3 * mean
    total = rstd * (gain * sb - PIX * mean_e - PIX * mean_en * centre)
    return sb, sx, sg, mean_en, c1, c2, c3, total


def second_back_kernel(
    groups,
    pc_ref,
    pd_ref,
    lifted_ref,
    im_ref,
    stat_ref,
    vec_ref,
    tin_ref,
    perm_ref,
    k_ref,
    field_ref,
    din_ref,
    dvec_ref,
    t1_ref,
    d_ref,
    low_ref,
):
    small = 8
    pc_ref, pd_ref = pc_ref.at[0], pd_ref.at[0]

    @pl.when(pl.program_id(0) == 0)
    def _():
        band_weights(k_ref.at[0], t1_ref, True)
        din_ref[...] = jnp.zeros_like(din_ref)
        dvec_ref[...] = jnp.zeros_like(dvec_ref)

    def vec(i):
        return vec_ref[i : i + 1, :]

    def stat(i):
        return stat_ref[0, i : i + 1, :]

    one = jnp.ones((1, C), f32)
    mean, mu, rstd = stat(0), stat(2), stat(3)
    sb, sx, sg, mean_en, c1, c2, c3, total = norm_back(
        pd_ref, t1_ref, lifted_ref, d_ref, mean, mean + vec(0), mu, rstd, one, vec(1), vec(2)
    )
    for j, y0 in chunks(small):
        at = slice(y0 * NS, (y0 + small) * NS)
        x = lifted_ref[0, j, at, :].astype(f32)
        g = pc_ref[j + 1, y0 + 1 : y0 + 1 + small].reshape(small * NS, C).astype(f32)
        low_ref[at, j * C : (j + 1) * C] = (g + (d_ref[j, at, :] * c1 + (x * c3 + c2))).astype(bf)
    dvec_ref[...] += jnp.concatenate([total, sg, sb, jnp.zeros((5, C), f32)], axis=0)

    din_ref[...] += jnp.dot(im_ref[0], low_ref[...], preferred_element_type=f32)
    back = lax.dot_general(
        tin_ref[...], low_ref[...], (((1,), (1,)), ((), ())), preferred_element_type=f32
    )
    stack = (
        pltpu.roll(back[0:48], ROWS - NS, 1) + back[48:96] + pltpu.roll(back[96:144], NS, 1)
    )
    lane = lax.broadcasted_iota(jnp.int32, (64, 128), 1) % NS

    def tall(jj):
        v = stack[jj * 8 : (jj + 1) * 8, :]
        return jnp.concatenate([v[:, i * 128 : (i + 1) * 128] for i in range(8)], axis=0)

    before, after = tall(0), tall(NJ + 1)
    before = jnp.where(lane == NS - 1, pltpu.roll(before, 15, 1), pltpu.roll(before, 127, 1))
    after = jnp.where(lane == 0, pltpu.roll(after, 128 - 15, 1), pltpu.roll(after, 1, 1))
    cols = [tall(j + 1) for j in range(NJ)]
    cols[3] = cols[3] + before
    cols[0] = cols[0] + after
    rows = jnp.concatenate(cols, axis=1).astype(bf)
    spread = lax.dot_general(
        rows, perm_ref[...], (((1,), (1,)), ((), ())), preferred_element_type=f32
    )
    natural = jnp.concatenate([spread[i * 8 : (i + 1) * 8, :] for i in range(8)], axis=1)
    cells = PIX // groups
    for g in range(groups):
        field_ref[g, 0] = natural[:, g * cells : (g + 1) * cells].astype(bf)


def whole(shape):
    return pl.BlockSpec(shape, lambda i, *_: (0,) * len(shape))


def by_item(shape, count=1, start=0):
    return pl.BlockSpec((count,) + shape, lambda i, *_: (i + start,) + (0,) * len(shape))


def swap(x, axis, hops):
    size = lax.axis_size(axis)
    return lax.ppermute(x, axis, [(i, (i + hops) % size) for i in range(size)])


def all_sum(x, axis, bit=1, end=None):
    size = lax.axis_size(axis)
    end = size if end is None else end
    while bit < end:
        x = x + lax.ppermute(x, axis, [(i, i ^ bit) for i in range(size)])
        bit *= 2
    return x


def local(
    fields,
    slot_mask,
    noise_step,
    cotangent,
    in_weight,
    in_moment,
    in_square,
    mid_weight,
    mid_moment,
    mid_square,
    time_weight,
    time_moment,
    time_square,
    vec_params,
    vec_moment,
    vec_square,
):
    both = ("wide", "grp")
    groups = lax.axis_size("grp")
    devices = groups * lax.axis_size("wide")
    held = fields.shape[0]
    items = held // groups
    slots = fields.shape[1]
    own = cotangent.shape[1]
    cells = fields.shape[2]
    me = lax.axis_index("grp")
    first_item = me * items
    pair = 2
    halves = 2
    some = items // halves

    mask_float = slot_mask.astype(f32)[:, :, None]
    masked_low = (fields * mask_float).astype(bf)

    def to_peer(x, hops, start, count, after=None):
        at = lax.rem(me + hops, groups) * items + start
        if after is not None:
            x, _ = lax.optimization_barrier((x, after))
        return swap(lax.dynamic_slice_in_dim(x, at, count, 0), "grp", hops)

    field_parts = [masked_low] + [to_peer(masked_low, s, 0, items) for s in range(1, groups)]
    share = mid_weight.shape[0]
    copies = jnp.broadcast_to(mid_weight.astype(bf)[None], (devices, share, C))
    gathered = lax.all_to_all(copies, both, split_axis=0, concat_axis=0, tiled=True)
    inner_taps = gathered.reshape(2, TAPS, C, C)
    cot_parts = [
        [
            to_peer(cotangent, s, h * some, some, field_parts[-1] if h > 0 else None)
            for s in range(1, groups)
        ]
        for h in range(halves)
    ]

    taps_in = in_weight.astype(bf).reshape(3, 3, slots, C)
    tin = jnp.stack(
        [jnp.pad(taps_in, ((0, 0), (j, NJ - 1 - j), (0, 0), (0, 0))) for j in range(NJ)], axis=3
    ).reshape(3 * (NJ + 2) * slots, NJ * C)
    spot = jnp.arange(8 * W)
    goal = (spot % NJ) * 128 + (spot // W) * NS + (spot % W) // NJ
    perm = (goal[:, None] == spot[None, :]).astype(bf)

    steps = lax.dynamic_slice_in_dim(noise_step, first_item, items, 0)
    features = fourier(steps, time_weight.shape[0])
    scaling = jnp.dot(features, time_weight[:, :C], precision=highest) + vec_params[4][None, :]
    offset = jnp.dot(features, time_weight[:, C:], precision=highest) + vec_params[5][None, :]
    item_vec = jnp.stack([1.0 + scaling, offset] + [jnp.zeros_like(offset)] * 6, axis=1)
    vecs = jnp.pad(vec_params, ((0, 7), (0, 0)))

    act = jax.ShapeDtypeStruct((items, NJ, ROWS, C), bf)
    flat = jax.ShapeDtypeStruct((items, 2, 2 * C, ROWS), bf)
    taps_rows = 3 * (NJ + 2) * slots
    pad_shape = (NJ + 2, H + 2, NS, C)
    pads = jax.ShapeDtypeStruct((items,) + pad_shape, bf)
    row = jax.ShapeDtypeStruct((items, 8, C), f32)
    band = pltpu.VMEM((12 * C, 2 * C), bf)
    tall = pltpu.VMEM((PIX, C), f32)
    params = pltpu.CompilerParams(vmem_limit_bytes=VMEM_LIMIT)
    my_group = me.astype(jnp.int32).reshape(1)

    def work(count, size, moved):
        gain = 2 * TAPS * C * C * PIX
        return pl.CostEstimate(
            flops=int(count * size * gain * 2),
            bytes_accessed=int(count * moved * 2 * C * PIX),
            transcendentals=0,
        )

    def mine(shape, count, index):
        return pl.BlockSpec(
            (count,) + shape, lambda i, g: (g[0] * (items // count) + index(i), 0, 0)
        )

    steps = items // pair
    early_steps = max(1, steps // 2)
    late_steps = max(1, steps - early_steps)
    early = early_steps * pair
    lifted, first_conv, x1t, x2t, im, stats, block_out, *sends = pl.pallas_call(
        functools.partial(forward_kernel, groups, early_steps),
        grid_spec=pltpu.PrefetchScalarGridSpec(
            num_scalar_prefetch=1,
            grid=(items // pair,),
            in_specs=[mine((slots, cells), pair, lambda i: i)]
            + [by_item((slots, cells), pair)] * (groups - 1)
            + [
                whole((8 * W, 8 * W)),
                whole((taps_rows, NJ * C)),
                whole((2, TAPS, C, C)),
                whole((16, C)),
                by_item((8, C), pair),
            ],
            out_specs=[
                by_item((NJ, ROWS, C), pair),
                by_item((NJ, ROWS, C), pair),
                by_item((2, 2 * C, ROWS), pair),
                by_item((2, 2 * C, ROWS), pair),
                by_item((taps_rows, ROWS), pair),
                by_item((8, C), pair),
                mine((own, PIX), pair, lambda i: i),
            ]
            + [
                pl.BlockSpec(
                    (pair, own, PIX), lambda i, g: (jnp.minimum(i, early_steps - 1), 0, 0)
                )
            ]
            * (groups - 1)
            + [
                pl.BlockSpec(
                    (pair, own, PIX), lambda i, g: (jnp.maximum(i - early_steps, 0), 0, 0)
                )
            ]
            * (groups - 1),
            scratch_shapes=[band] * 2 + [pltpu.VMEM(pad_shape, bf)] * 4 + [tall] * 2,
        ),
        out_shape=[
            act,
            act,
            flat,
            flat,
            jax.ShapeDtypeStruct((items, taps_rows, ROWS), bf),
            row,
            jax.ShapeDtypeStruct((held, own, PIX), f32),
        ]
        + [jax.ShapeDtypeStruct((early, own, PIX), bf)] * (groups - 1)
        + [jax.ShapeDtypeStruct((late_steps * pair, own, PIX), bf)] * (groups - 1),
        compiler_params=params,
        cost_estimate=work(items, 2.1, 7.5),
        name="forward_items",
    )(my_group, *field_parts, perm, tin, inner_taps, vecs, item_vec)

    sent = [[swap(sends[s - 1], "grp", s) for s in range(1, groups)]]
    late = sends[groups - 1 :] if early < items else []
    sent.append([swap(x, "grp", s + 1) for s, x in enumerate(late)])

    pc = pd = mid_grad = None
    mid_vecs = 0.0
    item_grads = []
    for h in range(halves):
        start = h * some
        chained = h > 0
        cot = [cotangent] + cot_parts[h]
        extra = [pc, pd, mid_grad] if chained else []
        any_spec = pl.BlockSpec(memory_space=pl.ANY)

        def after(i):
            return jnp.minimum(i + 1, some - 1)

        def cot_specs(index, start=start):
            return [mine((own, PIX), 1, lambda i: index(i) + start)] + [
                pl.BlockSpec((1, own, PIX), lambda i, g: (index(i), 0, 0))
            ] * (groups - 1)

        pc, pd, mid_grad, dvec, ditem = pl.pallas_call(
            functools.partial(first_back_kernel, groups, some, chained),
            grid_spec=pltpu.PrefetchScalarGridSpec(
                num_scalar_prefetch=1,
                grid=(some,),
                in_specs=cot_specs(lambda i: 0)
                + cot_specs(after)
                + [
                    by_item((NJ, ROWS, C), 1, start),
                    by_item((2, 2 * C, ROWS), 1, start),
                    by_item((2, 2 * C, ROWS), 1, start),
                    by_item((8, C), 1, start),
                    by_item((8, C), 1, start),
                    whole((16, C)),
                    whole((2, TAPS, C, C)),
                ]
                + ([any_spec, any_spec, whole((2, TAPS * C, C))] if chained else []),
                out_specs=[
                    by_item(pad_shape, 1, start),
                    by_item(pad_shape, 1, start),
                    whole((2, TAPS * C, C)),
                    whole((8, C)),
                    by_item((8, C), 1),
                ],
                scratch_shapes=[
                    band,
                    tall,
                    pltpu.VMEM((NJ, ROWS, C), f32),
                    pltpu.VMEM((2, 3, 2 * C, 4 * C), f32),
                ],
            ),
            out_shape=[
                pads,
                pads,
                jax.ShapeDtypeStruct((2, TAPS * C, C), f32),
                jax.ShapeDtypeStruct((8, C), f32),
                jax.ShapeDtypeStruct((some, 8, C), f32),
            ],
            input_output_aliases={2 * groups + 8: 0, 2 * groups + 9: 1} if chained else {},
            compiler_params=params,
            cost_estimate=work(some, 3.1, 7.2),
            name="first_back_items",
        )(my_group, *cot, *cot, first_conv, x1t, x2t, stats, item_vec, vecs, inner_taps, *extra)
        mid_vecs = mid_vecs + dvec
        item_grads.append(ditem)
    ditem = jnp.concatenate(item_grads, axis=0)

    wide = lax.axis_size("wide")
    small = jnp.concatenate([features, ditem[:, 0, :], ditem[:, 1, :], mid_vecs], axis=0)
    small = jnp.broadcast_to(small[None], (wide,) + small.shape)
    shares = groups * share
    parts = jnp.concatenate([mid_grad.reshape(wide, shares, C), small], axis=1)
    parts = lax.all_to_all(parts, "wide", split_axis=0, concat_axis=0, tiled=True)

    stats, sent[0] = lax.optimization_barrier((stats, sent[0]))
    field_low, din, outer_vecs = pl.pallas_call(
        functools.partial(second_back_kernel, groups),
        grid=(items,),
        out_shape=[
            jax.ShapeDtypeStruct((groups, items, slots, cells), bf),
            jax.ShapeDtypeStruct((taps_rows, NJ * C), f32),
            jax.ShapeDtypeStruct((8, C), f32),
        ],
        in_specs=[
            by_item(pad_shape),
            by_item(pad_shape),
            by_item((NJ, ROWS, C)),
            by_item((taps_rows, ROWS)),
            by_item((8, C)),
            whole((16, C)),
            whole((taps_rows, NJ * C)),
            whole((8 * W, 8 * W)),
            whole((2, TAPS, C, C)),
        ],
        out_specs=[
            pl.BlockSpec((groups, 1, slots, cells), lambda i: (0, i, 0, 0)),
            whole((taps_rows, NJ * C)),
            whole((8, C)),
        ],
        scratch_shapes=[
            band,
            pltpu.VMEM((NJ, ROWS, C), f32),
            pltpu.VMEM((ROWS, NJ * C), bf),
        ],
        compiler_params=params,
        cost_estimate=work(items, 1.2, 4.6),
        name="second_back_items",
    )(pc, pd, lifted, im, stats, vecs, tin, perm, inner_taps)

    din, parts = lax.optimization_barrier((din, parts))
    din = din.reshape(3, NJ + 2, slots, NJ, C)
    grad_in = sum(din[:, j : j + 3, :, j, :] for j in range(NJ)).reshape(TAPS * slots, C)
    small = parts[:, shares:]
    all_features = small[:, :items].reshape(wide * items, C)
    time_rows = [
        lax.dot_general(
            all_features,
            small[:, k * items : (k + 1) * items].reshape(wide * items, C),
            (((0,), (0,)), ((), ())),
            precision=highest,
        )
        for k in (1, 2)
    ]
    rows_all = jnp.concatenate(time_rows + [jnp.sum(small[:, 3 * items :], axis=0)], axis=0)
    partial = jnp.sum(parts[:, :shares], axis=0)
    last = all_sum(jnp.concatenate([grad_in, outer_vecs], axis=0), "wide", 1, 2)
    last, field_low, sent[0] = lax.optimization_barrier((last, field_low, sent[0]))
    field_grad = jnp.zeros((held, slots, cells), f32)
    for s in range(groups):
        source = lax.rem(me + groups - s, groups) * items
        block = lax.dynamic_index_in_dim(field_low, lax.rem(me + s, groups), 0, False)
        if s > 0:
            block = swap(block, "grp", s)
        field_grad = lax.dynamic_update_slice(field_grad, block.astype(f32), (source, 0, 0))
    field_grad = field_grad * mask_float

    last = all_sum(last, "wide", 2)
    rows_in = last.shape[0]
    last, sent[1] = lax.optimization_barrier((last, sent[1]))
    for start, arrived in ((0, sent[0]), (early, sent[1])):
        for s, block in enumerate(arrived):
            source = lax.rem(me + groups - s - 1, groups) * items
            block_out = lax.dynamic_update_slice(
                block_out, block.astype(f32), (source + start, 0, 0)
            )
    last = all_sum(jnp.concatenate([last, rows_all, partial], axis=0), "grp")
    rows_all = last[rows_in : rows_in + rows_all.shape[0]]
    time_total = jnp.concatenate([rows_all[:C], rows_all[C : 2 * C]], axis=1)
    mid_vecs = rows_all[2 * C :]
    partial = last[last.shape[0] - shares :].reshape(groups, share, C)
    mid_total = lax.dynamic_index_in_dim(partial, me, 0, False)
    last = last[:rows_in]
    in_total = last[: TAPS * slots]
    outer_vecs = last[TAPS * slots :]
    cot_row = mid_vecs[5:6]
    vec_total = jnp.concatenate(
        [outer_vecs[0:1] + cot_row, outer_vecs[1:3], mid_vecs[0:5], cot_row], axis=0
    )

    step_float = jnp.float32(STEP)
    in_new, in_first, in_second = adam_update(
        in_weight, in_total, in_moment, in_square, rate_in, step_float
    )
    mid_new, mid_first, mid_second = adam_update(
        mid_weight, mid_total, mid_moment, mid_square, rate_mid, step_float
    )
    time_new, time_first, time_second = adam_update(
        time_weight, time_total, time_moment, time_square, rate_time, step_float
    )
    vec_new, vec_first, vec_second = adam_update(
        vec_params, vec_total, vec_moment, vec_square, rate_vecs, step_float
    )
    return (
        block_out,
        field_grad,
        in_new,
        in_first,
        in_second,
        in_new.astype(bf),
        mid_new,
        mid_first,
        mid_second,
        mid_new.astype(bf),
        time_new,
        time_first,
        time_second,
        vec_new,
        vec_first,
        vec_second,
    )


def solution(mesh):
    rows = P(("wide", "grp"), None)
    return jax.shard_map(
        local,
        mesh=mesh,
        in_specs=(
            P("wide", None, "grp"),
            P("wide", None),
            P("wide"),
            P("wide", "grp", None),
            P(),
            P(),
            P(),
            rows,
            rows,
            rows,
            P(),
            P(),
            P(),
            P(),
            P(),
            P(),
        ),
        out_specs=(
            P("wide", "grp", None),
            P("wide", None, "grp"),
            P(),
            P(),
            P(),
            P(),
            rows,
            rows,
            rows,
            rows,
            P(),
            P(),
            P(),
            P(),
            P(),
            P(),
        ),
        check_vma=False,
    )
```
